512 devices in a mesh: expert: 64 (over x, z, core), dp: 8 (over y).
Axes of the slice: x: 4, y: 8, z: 8, core: 2. Of those that a mesh axis runs over, the one named last changes fastest.
Arguments:
- tokens: bfloat16 [65536, 2048], P(('expert', 'dp')), may hold values from -6 to 6
- upstream: bfloat16 [65536, 2048], P(('expert', 'dp')), may hold values from -6 to 6
- expert_ids: int32 [65536, 2], P(('expert', 'dp')), may hold values from 0 to 63, all different within a row; in each aligned block of 128 rows (0 to 127, 128 to 255, ...) at most 8 rows name the same one
- route_weight: bfloat16 [65536, 2], P(('expert', 'dp')), may hold values from 0.099609375 to 1
- placement: int32 [64], replicated, may hold values from 0 to 63, each once
- swap_pair: int32 [32], replicated, may hold values 0 or 1
- expert_state: bfloat16 [64, 2048, 1024], P('expert', 'dp'), may hold values from -0.125 to 0.125
- first_moment: bfloat16 [64, 2048, 1024], P('expert', 'dp'), may hold values from -60 to 60
- second_moment: bfloat16 [64, 2048, 1024], P('expert', 'dp'), may hold values from 10 to 1000
Outputs:
- token_grad: bfloat16 [65536, 2048], P(('expert', 'dp'))
- weight_grad: bfloat16 [65536, 2], P(('expert', 'dp'))
- new_state: bfloat16 [64, 2048, 1024], P('expert', 'dp')
- new_first: bfloat16 [64, 2048, 1024], P('expert', 'dp')
- new_second: bfloat16 [64, 2048, 1024], P('expert', 'dp')
The draws below stay inside these ranges and needn't reach their ends.
Inputs may be any that keep to these rules, and one draw needn't show every extreme that they name: `expert_ids`: among the rows of one device no expert is named by more than 8 routes, and some expert reaches 8; a token's 2 experts differ.
All inputs are finite; a program needn't handle non-finite values.
Results may differ from the reference program's by a relative error of at most 0.0075.
Values may be sent and summed in bfloat16 or wider, within the bound.
A program may use at most 64 MiB of HBM per device.

```python
import math
import jax
import jax.numpy as jnp
import numpy as np
from jax import lax

D = 2048
FF = 512
TOK_DEV = 128
TOPK = 2
EXPERTS = 64
CAP = 8
TOKENS = 65536
N_EXPERT = 64
N_DP = 8


def plant(array, key, smallest, high):
    longest = array.shape.index(max(array.shape))
    spots = []
    for shift in (0, 1):
        where = [jax.random.randint(jax.random.fold_in(key, axis), (), 0, length) for axis, length in enumerate(array.shape)]
        where[longest] = (where[longest] + shift) % array.shape[longest]
        spots.append(tuple(where))
    return array.at[spots[0]].set(smallest).at[spots[1]].set(high)


def block_levels(key, dims, shards, smallest, largest):
    def one(dim, shards_of):
        steps = jax.random.uniform(jax.random.fold_in(jax.random.fold_in(key, 6), dim), (shards_of,), jnp.float32, smallest / len(shards), largest / len(shards))
        return jnp.repeat(jnp.exp(steps), dims[dim] // shards_of).reshape((-1,) + (1,) * (len(dims) - dim - 1))

    level = one(*shards[0])
    for cut in shards[1:]:
        level = level * one(*cut)
    return level


def deal_out(key, own, number, rows, number_of, top, reach, lean):
    ranking = jax.random.permutation(key, number_of)
    crowded, ordinary = load_shares(number_of, rows * top, reach, lean, True), load_shares(number_of, rows * top, reach, lean, False)
    places = jnp.arange(number_of)

    def named(tallies, offset_by):
        used = int((tallies > 0).sum())
        fixed = max(1, used // 4)
        passed = fixed + (places - fixed + offset_by * (used - fixed)) % max(1, number_of - fixed)
        return jnp.zeros((number_of,), jnp.int32).at[ranking[jnp.where(places < fixed, places, passed)]].set(jnp.asarray(tallies, jnp.int32))

    tallies = jnp.where(number % 4 == 0, named(crowded, number // 4), named(ordinary, number - number // 4 - 1))
    mixed = jax.random.permutation(jax.random.fold_in(own, 3), number_of)
    source_of, receiver = mixed[0:number_of // 2 * 2:2], mixed[1:number_of // 2 * 2:2]
    slack = jnp.minimum(tallies[source_of] - 1, reach - tallies[receiver]) // 2
    slack = jnp.where((source_of == ranking[0]) | (receiver == ranking[0]) | (tallies[receiver] == 0), 0, jnp.maximum(slack, 0))
    passed = jax.random.randint(jax.random.fold_in(own, 4), (number_of // 2,), 0, 1 << 20) % (slack + 1)
    tallies = tallies.at[source_of].add(-passed).at[receiver].add(passed)
    items = jnp.searchsorted(jnp.cumsum(tallies), jnp.arange(rows * top), side="right").astype(jnp.int32)
    table = items.reshape(top, rows).T
    table = table[jax.random.permutation(jax.random.fold_in(own, 1), rows)]
    offset_by = jax.random.randint(jax.random.fold_in(own, 2), (rows, 1), 0, top)
    return jnp.take_along_axis(table, (jnp.arange(top)[None, :] + offset_by) % top, axis=1)


def load_shares(amount, total, limit, skew, full):
    weights = [(1 << 20) // math.isqrt(rank ** skew) + 1 for rank in range(1, amount + 1)]
    largest = limit if full else min(limit, max(-(-total // amount), total * weights[0] // sum(weights)))
    least = 1 if total - largest >= amount - 1 else 0
    holding, surplus = [largest] + [least] * (amount - 1), total - largest - least * (amount - 1)
    while surplus > 0:
        free = [i for i in range(1, amount) if holding[i] < largest] or [i for i in range(1, amount) if holding[i] < limit]
        pool, budget = sum([weights[i] for i in free]), surplus
        for i in free:
            more = min(limit - holding[i], max(1, budget * weights[i] // pool), surplus)
            holding[i] = holding[i] + more
            surplus = surplus - more
    return np.array(holding)


def normal_values(own_key, dims, scale, most, pieces=(), kind=jnp.bfloat16):
    array = scale * jax.random.normal(own_key, dims, jnp.float32)
    if pieces:
        array = array * block_levels(own_key, dims, pieces, -0.22, 0.18)
    return jnp.clip(array, -most, most).astype(kind)


def setup_inputs(seed: int = 0) -> dict:
    key_of = jax.random.split(jax.random.key(seed), 10)
    tokens = normal_values(key_of[0], (TOKENS, D), 1.0, 6.0, ((0, 512),))
    upstream = normal_values(key_of[1], (TOKENS, D), 1.0, 6.0, ((0, 512),))
    expert_ids_keys = jax.random.split(jax.random.fold_in(key_of[2], 1), TOKENS // TOK_DEV)
    expert_ids_turns = jax.random.permutation(jax.random.fold_in(key_of[2], 3), TOKENS // TOK_DEV)
    expert_ids = jax.vmap(lambda own, number: deal_out(jax.random.fold_in(key_of[2], 2), own, number, TOK_DEV, EXPERTS, TOPK, CAP, 2))(expert_ids_keys, expert_ids_turns).reshape((TOKENS, TOPK))
    route_weight = jnp.clip(jnp.exp(math.log(1.0) - 2.306499 * jax.random.uniform(key_of[3], (TOKENS, TOPK), jnp.float32) ** block_levels(key_of[3], (TOKENS, TOPK), ((0, 512),), -0.2, 0.2)), 0.099609375, 1.0).astype(jnp.bfloat16)
    placement = jax.random.permutation(key_of[4], EXPERTS).astype(jnp.int32)
    swap_pair = plant((jax.random.randint(key_of[5], (EXPERTS // 2,), 0, 2) < 1).astype(jnp.int32), jax.random.fold_in(key_of[5], 1), 0, 1)
    expert_state = normal_values(key_of[6], (EXPERTS, D, 2 * FF), D ** -0.5, 0.125, ((0, 64), (1, 8)))
    first_moment = normal_values(key_of[7], (EXPERTS, D, 2 * FF), 10.0, 60.0, ((0, 64), (1, 8)))
    second_moment = jnp.clip(jnp.exp(math.log(1000.0) - 4.6051702 * jax.random.uniform(key_of[8], (EXPERTS, D, 2 * FF), jnp.float32) ** block_levels(key_of[8], (EXPERTS, D, 2 * FF), ((0, 64), (1, 8)), -0.2, 0.2)), 10.0, 1000.0).astype(jnp.bfloat16)
    return {"tokens": tokens, "upstream": upstream, "expert_ids": expert_ids, "route_weight": route_weight, "placement": placement, "swap_pair": swap_pair, "expert_state": expert_state, "first_moment": first_moment, "second_moment": second_moment}


def silu_grad(value):
    sig = jax.nn.sigmoid(value)
    return sig * (1.0 + value * (1.0 - sig))

def reference(tokens, upstream, expert_ids, route_weight, placement, swap_pair, expert_state, first_moment, second_moment):
    f32 = jnp.float32
    bf16 = jnp.bfloat16
    half = N_EXPERT // 2
    lanes = jnp.arange(N_EXPERT, dtype=jnp.int32)
    source = jnp.where(swap_pair[lanes % half] == 1, lanes ^ half, lanes)
    state_now = expert_state[source]
    first_now = first_moment[source]
    second_now = second_moment[source]
    home = jnp.where(swap_pair[placement % half] == 1, placement ^ half, placement)
    routes = TOK_DEV * TOPK
    ids = expert_ids.reshape(N_EXPERT, N_DP, routes)
    onehot = (ids[..., None] == lanes[None, None, None, :]).astype(jnp.int32)
    slot = lax.optimization_barrier(jnp.sum((jnp.cumsum(onehot, 2) - onehot) * onehot, 3)).astype(jnp.int32)
    dest = home[ids]
    src = jnp.broadcast_to(jnp.arange(N_EXPERT, dtype=jnp.int32)[:, None, None], ids.shape)
    dp_idx = jnp.broadcast_to(jnp.arange(N_DP, dtype=jnp.int32)[None, :, None], ids.shape)
    local = jnp.broadcast_to(jnp.arange(routes, dtype=jnp.int32)[None, None, :], ids.shape)
    route_id = ((src * N_DP + dp_idx) * routes + local).astype(jnp.int32)
    total = TOKENS * TOPK
    table = jnp.full((N_EXPERT, N_DP, N_EXPERT * CAP), total, jnp.int32)
    table = table.at[dest, dp_idx, src * CAP + slot].set(route_id)
    zero_row = jnp.zeros((1, D), bf16)
    route_x = jnp.concatenate([jnp.repeat(tokens, TOPK, axis=0), zero_row], 0)
    route_y = jnp.concatenate([jnp.repeat(upstream, TOPK, axis=0), zero_row], 0)
    route_w = jnp.concatenate([route_weight.reshape(-1), jnp.zeros((1,), bf16)], 0)
    corr_one = 1.0 - math.exp(1000.0 * math.log(0.9))
    corr_two = 1.0 - math.exp(1000.0 * math.log(0.999))

    def per_slot(carry, j):
        dx_all, dw_all = carry
        index = table[j]
        xrows = route_x[index].astype(f32)
        yrows = route_y[index]
        wrows = route_w[index]
        full = state_now[j].astype(f32)
        w_up = full[:, :FF]
        w_down = full[:, FF:]
        hid = jnp.einsum('dmk,kf->dmf', xrows, w_up)
        act = jax.nn.silu(hid).astype(bf16)
        out = jnp.einsum('dmf,kf->dmk', act.astype(f32), w_down)
        slot_dw = lax.optimization_barrier(jnp.sum(yrows.astype(f32) * out, -1)).astype(bf16)
        grad_rows = (wrows.astype(f32)[..., None] * yrows.astype(f32)).astype(bf16)
        back = jnp.einsum('dmk,kf->dmf', grad_rows.astype(f32), w_down)
        dh = (back * silu_grad(hid)).astype(bf16)
        slot_dx = jnp.einsum('dmf,kf->dmk', dh.astype(f32), w_up).astype(bf16)
        g_up = jnp.einsum('dmk,dmf->dkf', xrows, dh.astype(f32))
        g_down = jnp.einsum('dmk,dmf->dkf', grad_rows.astype(f32), act.astype(f32))
        parts = jnp.concatenate([g_up, g_down], -1).astype(bf16)
        grad = lax.optimization_barrier(jnp.sum(parts.astype(f32), 0))
        m2 = 0.9 * first_now[j].astype(f32) + 0.1 * grad
        v2 = 0.999 * second_now[j].astype(f32) + 0.001 * grad * grad
        upd = m2 / corr_one / (jnp.sqrt(v2 / corr_two) + 1e-08)
        w_old = state_now[j].astype(f32)
        w_new = w_old - 0.001 * (upd + 0.1 * w_old)
        flat = index.reshape(-1)
        dx_all = dx_all.at[flat].set(slot_dx.reshape(-1, D))
        dw_all = dw_all.at[flat].set(slot_dw.reshape(-1))
        return ((dx_all, dw_all), (w_new.astype(bf16), m2.astype(bf16), v2.astype(bf16)))
    init = (jnp.zeros((total + 1, D), bf16), jnp.zeros((total + 1,), bf16))
    (dx_all, dw_all), (new_state, new_first, new_second) = lax.scan(per_slot, init, jnp.arange(N_EXPERT, dtype=jnp.int32))
    token_grad = lax.optimization_barrier(jnp.sum(dx_all[:total].reshape(TOKENS, TOPK, D).astype(f32), 1)).astype(bf16)
    weight_grad = dw_all[:total].reshape(TOKENS, TOPK)
    return (token_grad, weight_grad, new_state, new_first, new_second)
```

```python
import functools
import math

import jax
import jax.numpy as jnp
from jax import lax
from jax.experimental import pallas as pl
from jax.experimental.pallas import tpu as pltpu
from jax.sharding import PartitionSpec as P

corr_one = 1.0 - math.exp(1000.0 * math.log(0.9))
corr_two = 1.0 - math.exp(1000.0 * math.log(0.999))

NX, NZ, NC = 4, 8, 2
CAP = 8
LANES = 128
MESH = pl.DeviceIdType.MESH
F32 = jnp.float32
BF16 = jnp.bfloat16


def iota(shape, dim):
    return lax.broadcasted_iota(jnp.int32, shape, dim)


def tiles(total, tile, body):
    if total <= tile:
        body(0)
        return

    def step(i, carry):
        body(pl.multiple_of(i * tile, tile))
        return carry

    lax.fori_loop(0, total // tile, step, 0)


def kernel(
    sizes,
    tok, up, meta, homec, flag, w_in, m_in, v_in,
    tg, dwo, grad, w_sel, m_got, v_got,
    xa, ya, mt, w_got, wfull, sx, sy, rx, ry, act_all, dh_all,
    dxs, dr, sr, fr, rs_send, rs_recv,
    z_send, z_recv, mt_send, mt_recv, sw_send, sw_recv, y_send, y_recv,
    x_send, x_recv, r_send, r_recv, b_send, b_recv, rs_ssem, rs_rsem, local_sem,
):
    ny, rows, width, hidden, wide = sizes
    ng = NX * NC
    hz, hy = NZ // 2, ny // 2
    chunk = 2 * CAP * ng
    part = width // ny
    half_rows = rows // 2
    e = lax.axis_index("expert")
    d = lax.axis_index("dp")
    c = lax.rem(e, NC)
    z = lax.rem(e // NC, NZ)
    x = e // (NC * NZ)
    g = x * NC + c

    def zdev(k):
        return {"expert": (x * NZ + lax.rem(z + k + NZ, NZ)) * NC + c}

    def gdev(k):
        return {"expert": (lax.div(k, NC) * NZ + z) * NC + lax.rem(k, NC)}

    def ydev(k):
        return {"dp": lax.rem(d + k + ny, ny)}

    def remote(src, dst, ssem, rsem, dev):
        return pltpu.make_async_remote_copy(
            src_ref=src, dst_ref=dst, send_sem=ssem, recv_sem=rsem, device_id=dev, device_id_type=MESH
        )

    barrier = pltpu.get_barrier_semaphore()
    for k in range(1, NZ):
        pl.semaphore_signal(barrier, inc=1, device_id=zdev(k), device_id_type=MESH)
    for k in range(1, ng):
        pl.semaphore_signal(barrier, inc=1, device_id=gdev(lax.rem(g + k, ng)), device_id_type=MESH)
    for k in (1, -1):
        pl.semaphore_signal(barrier, inc=1, device_id=ydev(k), device_id_type=MESH)
    pl.semaphore_wait(barrier, NZ - 1 + ng - 1 + 2)

    own = (tok, up)
    every = (xa, ya)

    def z_copy(t, way, step, sending):
        sign = 1 if way == 0 else -1
        back = step - 1 if sending else step
        block = lax.rem(z - sign * back + 2 * NZ, NZ)
        start = pl.multiple_of(block * rows, rows)
        low, size = (0, rows) if step < hz else (way * half_rows, half_rows)
        dst = every[t].at[pl.ds(start + low, size)]
        src = own[t].at[pl.ds(low, size)] if step == 1 else dst
        return remote(src, dst, z_send.at[t, way, step - 1], z_recv.at[t, way, step - 1], zdev(sign))

    def z_start(t, step):
        for way in (0, 1):
            z_copy(t, way, step, True).start()

    def z_wait(t, step):
        for way in (0, 1):
            z_copy(t, way, step, False).wait_recv()

    half = NX * NZ * NC // 2
    partner = {"expert": lax.rem(e + half, 2 * half)}
    swaps = [
        remote(src, dst, sw_send.at[i], sw_recv.at[i], partner)
        for i, (src, dst) in enumerate(((w_in, w_got), (m_in, m_got), (v_in, v_got)))
    ]

    def y_copy(way, step, sending):
        sign = 1 if way == 0 else -1
        back = step - 1 if sending else step
        block = lax.rem(d - sign * back + 2 * ny, ny)
        start = pl.multiple_of(block * part, part)
        low, size = (0, part) if step < hy else (way * (part // 2), part // 2)
        ref = wfull.at[pl.ds(start + low, size)]
        return remote(ref, ref, y_send.at[way, step - 1], y_recv.at[way, step - 1], ydev(sign))

    def y_start(step):
        for way in (0, 1):
            y_copy(way, step, True).start()

    def y_wait(step):
        for way in (0, 1):
            y_copy(way, step, False).wait_recv()

    def mt_copy(k, sending):
        block = z if sending else lax.rem(z - k + NZ, NZ)
        ref = mt.at[pl.ds(pl.multiple_of(block * 8, 8), 8)]
        return remote(ref, ref, mt_send.at[k - 1], mt_recv.at[k - 1], zdev(k))

    def positions():
        experts = homec.shape[0]
        ids0, ids1 = meta[0:1, :], meta[1:2, :]
        each = iota((experts, rows), 0).astype(F32)
        one0, one1 = ids0 == each, ids1 == each
        named = jnp.where(one0 | one1, 1.0, 0.0).astype(BF16)
        before = jnp.where(iota((rows, rows), 0) < iota((rows, rows), 1), 1.0, 0.0).astype(BF16)
        earlier = jnp.dot(named, before, preferred_element_type=F32)
        place = homec[...] * CAP + earlier
        pos0 = jnp.sum(jnp.where(one0, place, 0.0), 0, keepdims=True)
        pos1 = jnp.sum(jnp.where(one1, place, 0.0), 0, keepdims=True)
        line = iota((8, rows), 0)
        tile = jnp.where(line == 0, pos0, jnp.where(line == 1, pos1, meta[...]))
        mt[pl.ds(pl.multiple_of(z * 8, 8), 8), :] = tile

    def sources(p):
        if p == 0:
            return z, lax.rem(z + hz, NZ)
        return lax.rem(z + p, NZ), lax.rem(z - p + NZ, NZ)

    def pack(p, t):
        line = iota((chunk, rows), 0)
        group, side, slot = line // (2 * CAP), (line // CAP) % 2, line % CAP
        aim = (((group // NC) * NZ + z) * NC + group % NC) * CAP + slot
        hots, starts = [], []
        for s, block in enumerate(sources(p)):
            tile = mt[pl.ds(pl.multiple_of(block * 8, 8), 8), :]
            want = jnp.where(side == s, aim, -1).astype(F32)
            hit0, hit1 = tile[0:1, :] == want, tile[1:2, :] == want
            if t == 0:
                hot = jnp.where(hit0 | hit1, 1.0, 0.0)
            else:
                hot = jnp.where(hit0, tile[2:3, :], 0.0) + jnp.where(hit1, tile[3:4, :], 0.0)
            hots.append(hot.astype(BF16))
            starts.append(pl.multiple_of(block * rows, rows))
        out, got, buf = (sx, rx, xa) if t == 0 else (sy, ry, ya)
        mine = pl.ds(pl.multiple_of(p * chunk + g * 2 * CAP, 2 * CAP), 2 * CAP)

        def body(start):
            cols = pl.ds(start, min(512, width))
            packed = jnp.dot(hots[0], buf[pl.ds(starts[0], rows), cols], preferred_element_type=F32)
            packed += jnp.dot(hots[1], buf[pl.ds(starts[1], rows), cols], preferred_element_type=F32)
            out[pl.ds(p * chunk, chunk), cols] = packed.astype(BF16)

        tiles(width, 512, body)
        got[mine, :] = out[mine, :]

    def x_copy(p, t, k, sending):
        other = lax.rem(g + k, ng) if sending else lax.rem(g - k + ng, ng)
        src, dst = ((sx, rx), (sy, ry))[t]
        there = pl.ds(pl.multiple_of(p * chunk + other * 2 * CAP, 2 * CAP), 2 * CAP)
        here = pl.ds(pl.multiple_of(p * chunk + g * 2 * CAP, 2 * CAP), 2 * CAP)
        if sending:
            return remote(src.at[there], dst.at[here], x_send.at[t, p, k - 1], x_recv.at[t, p, k - 1], gdev(other))
        return remote(src.at[here], dst.at[there], x_send.at[t, p, k - 1], x_recv.at[t, p, k - 1], gdev(other))

    def peers(body):
        def step(k, carry):
            body(k)
            return carry

        lax.fori_loop(1, ng, step, 0)

    def x_start(p, t):
        peers(lambda k: x_copy(p, t, k, True).start())

    def x_wait(p, t):
        peers(lambda k: x_copy(p, t, k, False).wait_recv())

    def compute(p):
        at = pl.ds(p * chunk, chunk)
        hid = jnp.dot(rx[at, :], wfull[:, 0:hidden], preferred_element_type=F32)
        sig = 1.0 / (1.0 + jnp.exp(-hid))
        act = (hid * sig).astype(BF16)
        back = jnp.dot(ry[at, :], wfull[:, hidden:], preferred_element_type=F32)
        dh = (back * (sig * (1.0 + hid * (1.0 - sig)))).astype(BF16)
        act_all[at, :] = act
        dh_all[at, :] = dh
        weighted = jnp.sum(act.astype(F32) * back, 1, keepdims=True)
        dxs[at, width:] = jnp.broadcast_to(weighted, (chunk, LANES)).astype(BF16)

        def body(start):
            tile = wfull[pl.ds(start, min(512, width)), 0:hidden]
            dx = lax.dot_general(dh_all[at, :], tile, (((1,), (1,)), ((), ())), preferred_element_type=F32)
            dxs[at, pl.ds(start, min(512, width))] = dx.astype(BF16)

        tiles(width, 512, body)
        mine = pl.ds(pl.multiple_of(p * chunk + g * 2 * CAP, 2 * CAP), 2 * CAP)
        dr[mine, :] = dxs[mine, :]

    def r_copy(p, k, sending):
        other = lax.rem(g + k, ng) if sending else lax.rem(g - k + ng, ng)
        there = pl.ds(pl.multiple_of(p * chunk + other * 2 * CAP, 2 * CAP), 2 * CAP)
        here = pl.ds(pl.multiple_of(p * chunk + g * 2 * CAP, 2 * CAP), 2 * CAP)
        if sending:
            return remote(dxs.at[there], dr.at[here], r_send.at[p, k - 1], r_recv.at[p, k - 1], gdev(other))
        return remote(dxs.at[here], dr.at[there], r_send.at[p, k - 1], r_recv.at[p, k - 1], gdev(other))

    def r_start(p):
        peers(lambda k: r_copy(p, k, True).start())

    side_rows = CAP * ng

    def b_copy(p, s, sending):
        away = hz if p == 0 else (p if s == 0 else -p)
        block = z if sending else lax.rem(z - away + NZ, NZ)
        src = sr.at[pl.ds((2 * p + s) * side_rows, side_rows)]
        dst = fr.at[pl.ds(pl.multiple_of(block * side_rows, side_rows), side_rows)]
        return remote(src, dst, b_send.at[p, s], b_recv.at[p, s], zdev(away))

    def relay(p):
        peers(lambda k: r_copy(p, k, False).wait_recv())
        to, frm = iota((chunk, chunk), 0), iota((chunk, chunk), 1)
        side, group, slot = to // side_rows, (to // CAP) % ng, to % CAP
        move = jnp.where(frm == group * 2 * CAP + side * CAP + slot, 1.0, 0.0).astype(BF16)

        def body(start, size=min(512, width)):
            cols = pl.ds(start, size)
            moved = jnp.dot(move, dr[pl.ds(p * chunk, chunk), cols], preferred_element_type=F32)
            sr[pl.ds(p * chunk, chunk), cols] = moved.astype(BF16)

        tiles(width, 512, body)
        body(width, LANES)
        if p == 0:
            fr[pl.ds(pl.multiple_of(z * side_rows, side_rows), side_rows), :] = sr[0:side_rows, :]
            b_copy(0, 1, True).start()
        else:
            for s in (0, 1):
                b_copy(p, s, True).start()

    def own_part(block, h):
        cols = pl.ds(pl.multiple_of(block * part, part), part)
        left, right = ((rx, dh_all), (ry, act_all))[h]
        return lax.dot_general(
            left[:, cols], right[...], (((0,), (0,)), ((), ())), preferred_element_type=F32
        )

    def rs_copy(way, step, h):
        sign = 1 if way == 0 else -1
        return remote(
            rs_send.at[way, step - 1, h], rs_recv.at[way, step - 1, h],
            rs_ssem.at[way, step - 1, h], rs_rsem.at[way, step - 1, h], ydev(sign),
        )

    def rs_halves(way, step):
        return (way,) if step == 1 else (0, 1)

    def rs_step(step):
        for h in (0, 1):
            for way in (0, 1):
                if h not in rs_halves(way, step):
                    continue
                sign = 1 if way == 0 else -1
                block = lax.rem(d + sign * (hy + 1 - step) + ny, ny)
                total = own_part(block, h)
                if step > 1 and h in rs_halves(way, step - 1):
                    rs_copy(way, step - 1, h).wait_recv()
                    total += rs_recv[way, step - 2, h].astype(F32)
                rs_send[way, step - 1, h] = total.astype(BF16)
                rs_copy(way, step, h).start()

    def rs_last():
        for h in (0, 1):
            total = own_part(d, h)
            for way in (0, 1):
                if h in rs_halves(way, hy):
                    rs_copy(way, hy, h).wait_recv()
                    total += rs_recv[way, hy - 1, h].astype(F32)
            grad[:, h * hidden : (h + 1) * hidden] = total

    def finish():
        for p in range(hz):
            for s in (0, 1):
                if (p, s) != (0, 0):
                    b_copy(p, s, False).wait_recv()
        tile = mt[pl.ds(pl.multiple_of(z * 8, 8), 8), :]
        lines = side_rows * NZ
        line = iota((lines, rows), 0)
        plane, group, slot = line // side_rows, (line // CAP) % ng, line % CAP
        want = ((((group // NC) * NZ + plane) * NC + group % NC) * CAP + slot).astype(F32)
        hit0, hit1 = tile[0:1, :] == want, tile[1:2, :] == want
        both = jnp.where(hit0 | hit1, 1.0, 0.0).astype(BF16)
        dims = (((0,), (0,)), ((), ()))

        def body(start):
            cols = pl.ds(start, min(512, width))
            tg[:, cols] = lax.dot_general(both, fr[:, cols], dims, preferred_element_type=F32).astype(BF16)

        tiles(width, 512, body)
        lane = iota((rows, LANES), 1)
        sums = [
            lax.dot_general(
                jnp.where(hit, 1.0, 0.0).astype(BF16), fr[:, width:], dims, preferred_element_type=F32
            )
            for hit in (hit0, hit1)
        ]
        dwo[...] = jnp.where(lane == 0, sums[0], sums[1])

    z_start(0, 1)
    swaps[0].start()
    z_start(1, 1)
    positions()
    for k in range(1, NZ):
        mt_copy(k, True).start()
    xa[pl.ds(pl.multiple_of(z * rows, rows), rows), :] = tok[...]
    ya[pl.ds(pl.multiple_of(z * rows, rows), rows), :] = up[...]

    def state_in():
        swaps[0].wait_recv()
        here = pl.ds(pl.multiple_of(d * part, part), part)
        chosen = jnp.where(flag[0:1, :] == 1.0, w_got[...].astype(F32), w_in[...].astype(F32)).astype(BF16)
        wfull[here, :] = chosen
        w_sel[...] = chosen
        y_start(1)
        swaps[1].start()
        swaps[2].start()

    def metas_in():
        for k in range(1, NZ):
            mt_copy(k, False).wait_recv()

    done_y = 0
    for step in range(1, hz + 1):
        for t in (0, 1):
            z_wait(t, step)
            if step < hz:
                z_start(t, step + 1)
            if step == 1 and t == 0:
                state_in()
                metas_in()
        if step < hz:
            if step <= hy:
                y_wait(step)
                done_y = step
                if step < hy:
                    y_start(step + 1)
            for t in (0, 1):
                pack(step, t)
                x_start(step, t)
    while done_y < hy:
        done_y += 1
        y_wait(done_y)
        if done_y < hy:
            y_start(done_y + 1)
    for t in (0, 1):
        pack(0, t)
        x_start(0, t)
    for p in list(range(1, hz)) + [0]:
        for t in (0, 1):
            x_wait(p, t)
        compute(p)
        r_start(p)
    rs_step(1)
    for p in list(range(1, hz)):
        relay(p)
    if hy > 1:
        rs_step(2)
    relay(0)
    for step in range(3, hy + 1):
        rs_step(step)
    finish()
    rs_last()

    for t in (0, 1):
        for way in (0, 1):
            for step in range(1, hz + 1):
                z_copy(t, way, step, True).wait_send()
    for way in (0, 1):
        for step in range(1, hy + 1):
            y_copy(way, step, True).wait_send()
            for h in rs_halves(way, step):
                rs_copy(way, step, h).wait_send()
    for k in range(1, NZ):
        mt_copy(k, True).wait_send()
    for p in range(hz):
        for t in (0, 1):
            peers(lambda k: x_copy(p, t, k, True).wait_send())
        peers(lambda k: r_copy(p, k, True).wait_send())
        for s in (0, 1):
            if (p, s) != (0, 0):
                b_copy(p, s, True).wait_send()
    swaps[0].wait_send()
    for i in (1, 2):
        swaps[i].wait()


def exchange(tokens, upstream, meta, homec, flag, w_in, m_in, v_in):
    ny = lax.axis_size("dp")
    rows, width = tokens.shape
    part, both = w_in.shape
    hidden = both // 2
    ng = NX * NC
    hz, hy = NZ // 2, ny // 2
    chunk = 2 * CAP * ng
    lines = hz * chunk
    wide = width + LANES
    vmem = pl.BlockSpec(memory_space=pltpu.VMEM)
    any_ = pl.BlockSpec(memory_space=pl.ANY)
    dma = pltpu.SemaphoreType.DMA
    return pl.pallas_call(
        functools.partial(kernel, (ny, rows, width, hidden, wide)),
        name="exchange",
        out_shape=(
            jax.ShapeDtypeStruct((rows, width), BF16),
            jax.ShapeDtypeStruct((rows, LANES), F32),
            jax.ShapeDtypeStruct((part, both), F32),
            jax.ShapeDtypeStruct((part, both), BF16),
            jax.ShapeDtypeStruct((part, both), BF16),
            jax.ShapeDtypeStruct((part, both), BF16),
        ),
        in_specs=[vmem] * 6 + [any_] * 2,
        out_specs=(vmem,) * 4 + (any_,) * 2,
        scratch_shapes=[
            pltpu.VMEM((NZ * rows, width), BF16),
            pltpu.VMEM((NZ * rows, width), BF16),
            pltpu.VMEM((NZ * 8, rows), F32),
            pltpu.VMEM((part, both), BF16),
            pltpu.VMEM((width, both), BF16),
            pltpu.VMEM((lines, width), BF16),
            pltpu.VMEM((lines, width), BF16),
            pltpu.VMEM((lines, width), BF16),
            pltpu.VMEM((lines, width), BF16),
            pltpu.VMEM((lines, hidden), BF16),
            pltpu.VMEM((lines, hidden), BF16),
            pltpu.VMEM((lines, wide), BF16),
            pltpu.VMEM((lines, wide), BF16),
            pltpu.VMEM((lines, wide), BF16),
            pltpu.VMEM((lines, wide), BF16),
            pltpu.VMEM((2, hy, 2, part, hidden), BF16),
            pltpu.VMEM((2, hy, 2, part, hidden), BF16),
            dma((2, 2, hz)), dma((2, 2, hz)),
            dma((NZ - 1,)), dma((NZ - 1,)),
            dma((3,)), dma((3,)),
            dma((2, hy)), dma((2, hy)),
            dma((2, hz, ng - 1)), dma((2, hz, ng - 1)),
            dma((hz, ng - 1)), dma((hz, ng - 1)),
            dma((hz, 2)), dma((hz, 2)),
            dma((2, hy, 2)), dma((2, hy, 2)),
            dma((1,)),
        ],
        compiler_params=pltpu.CompilerParams(
            collective_id=0, has_side_effects=True, vmem_limit_bytes=60 * 1024 * 1024
        ),
    )(tokens, upstream, meta, homec, flag, w_in, m_in, v_in)


def adam_update(weights, first, second, grad):
    m_next = 0.9 * first.astype(F32) + 0.1 * grad
    v_next = 0.999 * second.astype(F32) + 0.001 * grad * grad
    update = m_next / corr_one / (jnp.sqrt(v_next / corr_two) + 1e-08)
    w_old = weights.astype(F32)
    w_next = w_old - 0.001 * (update + 0.1 * w_old)
    return w_next.astype(BF16), m_next.astype(BF16), v_next.astype(BF16)


def shards(
    tokens,
    upstream,
    expert_ids,
    route_weight,
    placement,
    swap_pair,
    expert_state,
    first_moment,
    second_moment,
):
    lanes_count = lax.axis_size("expert")
    half = lanes_count // 2
    rows, top = expert_ids.shape
    both = expert_state.shape[2]
    halves = jnp.arange(half, dtype=jnp.int32)
    own_index = lax.axis_index("expert")
    own_flag = jnp.sum(jnp.where(halves == own_index % half, swap_pair, 0))
    match_half = (placement % half)[:, None] == halves[None, :]
    moved = jnp.sum(jnp.where(match_half, swap_pair[None, :], 0), 1)
    home = jnp.where(moved == 1, placement ^ half, placement)
    homec = jnp.broadcast_to(home.astype(F32)[:, None], (lanes_count, rows))
    flag = jnp.broadcast_to(own_flag.astype(F32), (8, both))
    meta = jnp.concatenate(
        [expert_ids.T.astype(F32), route_weight.T.astype(F32), jnp.zeros((8 - 2 * top, rows), F32)], 0
    )
    token_grad, weighted, grad, w_sel, m_got, v_got = exchange(
        tokens, upstream, meta, homec, flag, expert_state[0], first_moment[0], second_moment[0]
    )
    weight_grad = (weighted[:, :top] / route_weight.astype(F32)).astype(BF16)
    swapped = own_flag == 1
    m_sel = jnp.where(swapped, m_got, first_moment[0])
    v_sel = jnp.where(swapped, v_got, second_moment[0])
    w_new, m_new, v_new = adam_update(w_sel, m_sel, v_sel, grad)
    return (token_grad, weight_grad, w_new[None], m_new[None], v_new[None])


def solution(mesh):
    in_specs = (
        P(("expert", "dp"), None),
        P(("expert", "dp"), None),
        P(("expert", "dp"), None),
        P(("expert", "dp"), None),
        P(),
        P(),
        P("expert", "dp", None),
        P("expert", "dp", None),
        P("expert", "dp", None),
    )
    out_specs = (
        P(("expert", "dp"), None),
        P(("expert", "dp"), None),
        P("expert", "dp", None),
        P("expert", "dp", None),
        P("expert", "dp", None),
    )
    return jax.shard_map(shards, mesh=mesh, in_specs=in_specs, out_specs=out_specs, check_vma=False)
```

```python
import functools
import math

import jax
import jax.numpy as jnp
from jax import lax
from jax.experimental import pallas as pl
from jax.experimental.pallas import tpu as pltpu
from jax.sharding import PartitionSpec as P

corr_one = 1.0 - math.exp(1000.0 * math.log(0.9))
corr_two = 1.0 - math.exp(1000.0 * math.log(0.999))

NX, NZ, NC = 4, 8, 2
CAP = 8
LANES = 128
MESH = pl.DeviceIdType.MESH
F32 = jnp.float32
BF16 = jnp.bfloat16


def iota(shape, dim):
    return lax.broadcasted_iota(jnp.int32, shape, dim)


def tiles(total, tile, body):
    if total <= tile:
        body(0)
        return

    def step(i, carry):
        body(pl.multiple_of(i * tile, tile))
        return carry

    lax.fori_loop(0, total // tile, step, 0)


def kernel(
    sizes,
    tok, up, meta, homec, flag, w_in, m_in, v_in,
    tg, dwo, grad, w_sel, m_got, v_got,
    xa, ya, p3, r3, r4, mt, w_got, wfull, sx, sy, rx, ry, act_all, dh_all,
    dxs, dr, sr, fr, rs_send, rs_recv,
    z_send, z_recv, mt_send, mt_recv, sw_send, sw_recv, y_send, y_recv,
    x_send, x_recv, r_send, r_recv, b_send, b_recv, rs_ssem, rs_rsem, local_sem,
):
    ny, rows, width, hidden, wide = sizes
    ng = NX * NC
    hz, hy = NZ // 2, ny // 2
    chunk = 2 * CAP * ng
    part = width // ny
    e = lax.axis_index("expert")
    d = lax.axis_index("dp")
    c = lax.rem(e, NC)
    z = lax.rem(e // NC, NZ)
    x = e // (NC * NZ)
    g = x * NC + c

    def zdev(k):
        return {"expert": (x * NZ + lax.rem(z + k + NZ, NZ)) * NC + c}

    def gdev(k):
        return {"expert": (lax.div(k, NC) * NZ + z) * NC + lax.rem(k, NC)}

    def ydev(k):
        return {"dp": lax.rem(d + k + ny, ny)}

    def remote(src, dst, ssem, rsem, dev):
        return pltpu.make_async_remote_copy(
            src_ref=src, dst_ref=dst, send_sem=ssem, recv_sem=rsem, device_id=dev, device_id_type=MESH
        )

    barrier = pltpu.get_barrier_semaphore()
    for k in range(1, NZ):
        pl.semaphore_signal(barrier, inc=1, device_id=zdev(k), device_id_type=MESH)
    for k in range(1, ng):
        pl.semaphore_signal(barrier, inc=1, device_id=gdev(lax.rem(g + k, ng)), device_id_type=MESH)
    for k in (1, -1):
        pl.semaphore_signal(barrier, inc=1, device_id=ydev(k), device_id_type=MESH)
    pl.semaphore_wait(barrier, NZ - 1 + ng - 1 + 2)

    own = (tok, up)
    every = (xa, ya)

    side_rows = CAP * ng
    split = side_rows // 2

    def z_copy(t, way, step, sending):
        sign = 1 if way == 0 else -1
        sems = z_send.at[t, way, step - 1], z_recv.at[t, way, step - 1]
        if step == hz:
            return remote(
                r3.at[t, way, pl.ds(side_rows, split)], r4.at[t, pl.ds(way * split, split)], *sems, zdev(sign)
            )
        if step == hz - 1:
            return remote(p3.at[t, way], r3.at[t, way], *sems, zdev(sign))
        back = step - 1 if sending else step
        block = lax.rem(z - sign * back + 2 * NZ, NZ)
        dst = every[t].at[pl.ds(pl.multiple_of(block * rows, rows), rows)]
        return remote(own[t] if step == 1 else dst, dst, *sems, zdev(sign))

    def z_start(t, step):
        for way in (0, 1):
            z_copy(t, way, step, True).start()

    def z_wait(t, step):
        for way in (0, 1):
            z_copy(t, way, step, False).wait_recv()

    half = NX * NZ * NC // 2
    partner = {"expert": lax.rem(e + half, 2 * half)}
    swaps = [
        remote(src, dst, sw_send.at[i], sw_recv.at[i], partner)
        for i, (src, dst) in enumerate(((w_in, w_got), (m_in, m_got), (v_in, v_got)))
    ]

    def y_copy(way, step, sending):
        sign = 1 if way == 0 else -1
        back = step - 1 if sending else step
        block = lax.rem(d - sign * back + 2 * ny, ny)
        start = pl.multiple_of(block * part, part)
        low, size = (0, part) if step < hy else (way * (part // 2), part // 2)
        ref = wfull.at[pl.ds(start + low, size)]
        return remote(ref, ref, y_send.at[way, step - 1], y_recv.at[way, step - 1], ydev(sign))

    def y_start(step):
        for way in (0, 1):
            y_copy(way, step, True).start()

    def y_wait(step):
        for way in (0, 1):
            y_copy(way, step, False).wait_recv()

    def mt_copy(k, sending):
        block = z if sending else lax.rem(z - k + NZ, NZ)
        ref = mt.at[pl.ds(pl.multiple_of(block * 8, 8), 8)]
        return remote(ref, ref, mt_send.at[k - 1], mt_recv.at[k - 1], zdev(k))

    def positions():
        experts = homec.shape[0]
        ids0, ids1 = meta[0:1, :], meta[1:2, :]
        each = iota((experts, rows), 0).astype(F32)
        one0, one1 = ids0 == each, ids1 == each
        named = jnp.where(one0 | one1, 1.0, 0.0).astype(BF16)
        before = jnp.where(iota((rows, rows), 0) < iota((rows, rows), 1), 1.0, 0.0).astype(BF16)
        earlier = jnp.dot(named, before, preferred_element_type=F32)
        place = homec[...] * CAP + earlier
        pos0 = jnp.sum(jnp.where(one0, place, 0.0), 0, keepdims=True)
        pos1 = jnp.sum(jnp.where(one1, place, 0.0), 0, keepdims=True)
        line = iota((8, rows), 0)
        tile = jnp.where(line == 0, pos0, jnp.where(line == 1, pos1, meta[...]))
        mt[pl.ds(pl.multiple_of(z * 8, 8), 8), :] = tile

    def sources(p):
        if p == 0:
            return z, lax.rem(z + hz, NZ)
        return lax.rem(z + p, NZ), lax.rem(z - p + NZ, NZ)

    def hot_rows(block, want, t):
        tile = mt[pl.ds(pl.multiple_of(block * 8, 8), 8), :]
        want = want.astype(F32)
        hit0, hit1 = tile[0:1, :] == want, tile[1:2, :] == want
        if t == 0:
            hot = jnp.where(hit0 | hit1, 1.0, 0.0)
        else:
            hot = jnp.where(hit0, tile[2:3, :], 0.0) + jnp.where(hit1, tile[3:4, :], 0.0)
        return hot.astype(BF16)

    def pack_ahead(t):
        lines = side_rows + split
        line = iota((lines, rows), 0)
        for way in (0, 1):
            sign = 1 if way == 0 else -1
            block = lax.rem(z - sign * (hz - 2) + NZ, NZ)
            later = line >= side_rows
            inner = jnp.where(later, line - side_rows + way * split, line)
            group, slot = inner // CAP, inner % CAP
            near, far = lax.rem(z + sign + NZ, NZ), lax.rem(z + 2 * sign + NZ, NZ)
            plane = jnp.where(later, far, near)
            hot = hot_rows(block, (((group // NC) * NZ + plane) * NC + group % NC) * CAP + slot, t)
            start = pl.multiple_of(block * rows, rows)

            def body(at):
                cols = pl.ds(at, min(512, width))
                p3[t, way, :, cols] = jnp.dot(
                    hot, every[t][pl.ds(start, rows), cols], preferred_element_type=F32
                ).astype(BF16)

            tiles(width, 512, body)

    def pack(p, t):
        line = iota((chunk, rows), 0)
        group, side, slot = line // (2 * CAP), (line // CAP) % 2, line % CAP
        aim = (((group // NC) * NZ + z) * NC + group % NC) * CAP + slot
        few = iota((chunk, side_rows), 0)
        spot = (few // (2 * CAP)) * CAP + few % CAP
        few_side = (few // CAP) % 2
        hots, lefts = [], []
        for s, block in enumerate(sources(p)):
            if p == hz - 1 or (p == 0 and s == 1):
                hit = (iota((chunk, side_rows), 1) == spot) & (few_side == s)
                hots.append(jnp.where(hit, 1.0, 0.0).astype(BF16))
                lefts.append(r4.at[t] if p == 0 else r3.at[t, 1 - s, pl.ds(0, side_rows)])
            else:
                hots.append(hot_rows(block, jnp.where(side == s, aim, -1), t))
                lefts.append(every[t].at[pl.ds(pl.multiple_of(block * rows, rows), rows)])
        out, got = ((sx, rx), (sy, ry))[t]
        mine = pl.ds(pl.multiple_of(p * chunk + g * 2 * CAP, 2 * CAP), 2 * CAP)

        def body(start):
            cols = pl.ds(start, min(512, width))
            packed = jnp.dot(hots[0], lefts[0][:, cols], preferred_element_type=F32)
            packed += jnp.dot(hots[1], lefts[1][:, cols], preferred_element_type=F32)
            out[pl.ds(p * chunk, chunk), cols] = packed.astype(BF16)

        tiles(width, 512, body)
        got[mine, :] = out[mine, :]

    def x_copy(p, t, k, sending):
        other = lax.rem(g + k, ng) if sending else lax.rem(g - k + ng, ng)
        src, dst = ((sx, rx), (sy, ry))[t]
        there = pl.ds(pl.multiple_of(p * chunk + other * 2 * CAP, 2 * CAP), 2 * CAP)
        here = pl.ds(pl.multiple_of(p * chunk + g * 2 * CAP, 2 * CAP), 2 * CAP)
        if sending:
            return remote(src.at[there], dst.at[here], x_send.at[t, p, k - 1], x_recv.at[t, p, k - 1], gdev(other))
        return remote(src.at[here], dst.at[there], x_send.at[t, p, k - 1], x_recv.at[t, p, k - 1], gdev(other))

    def peers(body):
        def step(k, carry):
            body(k)
            return carry

        lax.fori_loop(1, ng, step, 0)

    def x_start(p, t):
        peers(lambda k: x_copy(p, t, k, True).start())

    def x_wait(p, t):
        peers(lambda k: x_copy(p, t, k, False).wait_recv())

    def compute(p):
        at = pl.ds(p * chunk, chunk)
        hid = jnp.dot(rx[at, :], wfull[:, 0:hidden], preferred_element_type=F32)
        sig = 1.0 / (1.0 + jnp.exp(-hid))
        act = (hid * sig).astype(BF16)
        back = jnp.dot(ry[at, :], wfull[:, hidden:], preferred_element_type=F32)
        dh = (back * (sig * (1.0 + hid * (1.0 - sig)))).astype(BF16)
        act_all[at, :] = act
        dh_all[at, :] = dh
        weighted = jnp.sum(act.astype(F32) * back, 1, keepdims=True)
        dxs[at, width:] = jnp.broadcast_to(weighted, (chunk, LANES)).astype(BF16)

        def body(start):
            tile = wfull[pl.ds(start, min(512, width)), 0:hidden]
            dx = lax.dot_general(dh_all[at, :], tile, (((1,), (1,)), ((), ())), preferred_element_type=F32)
            dxs[at, pl.ds(start, min(512, width))] = dx.astype(BF16)

        tiles(width, 512, body)
        mine = pl.ds(pl.multiple_of(p * chunk + g * 2 * CAP, 2 * CAP), 2 * CAP)
        dr[mine, :] = dxs[mine, :]

    def r_copy(p, k, sending):
        other = lax.rem(g + k, ng) if sending else lax.rem(g - k + ng, ng)
        there = pl.ds(pl.multiple_of(p * chunk + other * 2 * CAP, 2 * CAP), 2 * CAP)
        here = pl.ds(pl.multiple_of(p * chunk + g * 2 * CAP, 2 * CAP), 2 * CAP)
        if sending:
            return remote(dxs.at[there], dr.at[here], r_send.at[p, k - 1], r_recv.at[p, k - 1], gdev(other))
        return remote(dxs.at[here], dr.at[there], r_send.at[p, k - 1], r_recv.at[p, k - 1], gdev(other))

    def r_start(p):
        peers(lambda k: r_copy(p, k, True).start())

    def b_copy(p, s, sending):
        away = hz if p == 0 else (p if s == 0 else -p)
        block = z if sending else lax.rem(z - away + NZ, NZ)
        src = sr.at[pl.ds((2 * p + s) * side_rows, side_rows)]
        dst = fr.at[pl.ds(pl.multiple_of(block * side_rows, side_rows), side_rows)]
        return remote(src, dst, b_send.at[p, s], b_recv.at[p, s], zdev(away))

    def r_wait(p):
        peers(lambda k: r_copy(p, k, False).wait_recv())

    def relay(p):
        r_wait(p)
        to, frm = iota((chunk, chunk), 0), iota((chunk, chunk), 1)
        side, group, slot = to // side_rows, (to // CAP) % ng, to % CAP
        move = jnp.where(frm == group * 2 * CAP + side * CAP + slot, 1.0, 0.0).astype(BF16)

        def body(start, size=min(512, width)):
            cols = pl.ds(start, size)
            moved = jnp.dot(move, dr[pl.ds(p * chunk, chunk), cols], preferred_element_type=F32)
            sr[pl.ds(p * chunk, chunk), cols] = moved.astype(BF16)

        tiles(width, 512, body)
        body(width, LANES)
        if p == 0:
            fr[pl.ds(pl.multiple_of(z * side_rows, side_rows), side_rows), :] = sr[0:side_rows, :]
            b_copy(0, 1, True).start()
        else:
            for s in (0, 1):
                b_copy(p, s, True).start()

    def own_part(block, h):
        cols = pl.ds(pl.multiple_of(block * part, part), part)
        left, right = ((rx, dh_all), (ry, act_all))[h]
        return lax.dot_general(
            left[:, cols], right[...], (((0,), (0,)), ((), ())), preferred_element_type=F32
        )

    def rs_copy(way, step, h):
        sign = 1 if way == 0 else -1
        return remote(
            rs_send.at[way, step - 1, h], rs_recv.at[way, step - 1, h],
            rs_ssem.at[way, step - 1, h], rs_rsem.at[way, step - 1, h], ydev(sign),
        )

    def rs_halves(way, step):
        return (way,) if step == 1 else (0, 1)

    def rs_step(step):
        for h in (0, 1):
            for way in (0, 1):
                if h not in rs_halves(way, step):
                    continue
                sign = 1 if way == 0 else -1
                block = lax.rem(d + sign * (hy + 1 - step) + ny, ny)
                total = own_part(block, h)
                if step > 1 and h in rs_halves(way, step - 1):
                    rs_copy(way, step - 1, h).wait_recv()
                    total += rs_recv[way, step - 2, h].astype(F32)
                rs_send[way, step - 1, h] = total.astype(BF16)
                rs_copy(way, step, h).start()

    def rs_last():
        for h in (0, 1):
            total = own_part(d, h)
            for way in (0, 1):
                if h in rs_halves(way, hy):
                    rs_copy(way, hy, h).wait_recv()
                    total += rs_recv[way, hy - 1, h].astype(F32)
            grad[:, h * hidden : (h + 1) * hidden] = total

    def finish():
        for p in range(hz):
            for s in (0, 1):
                if (p, s) != (0, 0):
                    b_copy(p, s, False).wait_recv()
        tile = mt[pl.ds(pl.multiple_of(z * 8, 8), 8), :]
        lines = side_rows * NZ
        line = iota((lines, rows), 0)
        plane, group, slot = line // side_rows, (line // CAP) % ng, line % CAP
        want = ((((group // NC) * NZ + plane) * NC + group % NC) * CAP + slot).astype(F32)
        hit0, hit1 = tile[0:1, :] == want, tile[1:2, :] == want
        both = jnp.where(hit0 | hit1, 1.0, 0.0).astype(BF16)
        dims = (((0,), (0,)), ((), ()))

        def body(start):
            cols = pl.ds(start, min(512, width))
            tg[:, cols] = lax.dot_general(both, fr[:, cols], dims, preferred_element_type=F32).astype(BF16)

        tiles(width, 512, body)
        lane = iota((rows, LANES), 1)
        sums = [
            lax.dot_general(
                jnp.where(hit, 1.0, 0.0).astype(BF16), fr[:, width:], dims, preferred_element_type=F32
            )
            for hit in (hit0, hit1)
        ]
        dwo[...] = jnp.where(lane == 0, sums[0], sums[1])

    def metas_in():
        for k in range(1, NZ):
            mt_copy(k, False).wait_recv()

    def state_in():
        swaps[0].wait_recv()
        here = pl.ds(pl.multiple_of(d * part, part), part)
        chosen = jnp.where(flag[0:1, :] == 1.0, w_got[...].astype(F32), w_in[...].astype(F32)).astype(BF16)
        wfull[here, :] = chosen
        w_sel[...] = chosen
        y_start(1)
        swaps[1].start()
        swaps[2].start()

    def y_next(step):
        if step <= hy:
            y_wait(step)
            if step < hy:
                y_start(step + 1)

    def first_copies():
        positions()
        for k in range(1, NZ):
            mt_copy(k, True).start()
        xa[pl.ds(pl.multiple_of(z * rows, rows), rows), :] = tok[...]
        ya[pl.ds(pl.multiple_of(z * rows, rows), rows), :] = up[...]

    def send_on(t, step):
        if step == hz - 1:
            pack_ahead(t)
        z_start(t, step)

    swaps[0].start()
    if hz > 2:
        z_start(0, 1)
        z_start(1, 1)
        first_copies()
    else:
        first_copies()
        metas_in()
        send_on(0, 1)
        send_on(1, 1)
    done_y = 0
    for step in range(1, hz - 1):
        z_wait(0, step)
        if step == 1:
            metas_in()
        send_on(0, step + 1)
        if step == 1:
            state_in()
        else:
            done_y += 1
            y_next(done_y)
        z_wait(1, step)
        send_on(1, step + 1)
        for t in (0, 1):
            pack(step, t)
            x_start(step, t)
        done_y += 1
        y_next(done_y)
    if hz == 2:
        state_in()
    while done_y < hy:
        done_y += 1
        y_next(done_y)

    def work(p):
        for t in (0, 1):
            x_wait(p, t)
        compute(p)
        r_start(p)

    early = list(range(1, hz - 1))
    if early:
        work(early[0])
    z_wait(0, hz - 1)
    z_start(0, hz)
    pack(hz - 1, 0)
    x_start(hz - 1, 0)
    for p in early[1:]:
        work(p)
    z_wait(1, hz - 1)
    z_start(1, hz)
    pack(hz - 1, 1)
    x_start(hz - 1, 1)
    for t in (0, 1):
        z_wait(t, hz)
        pack(0, t)
        x_start(0, t)
    for p in early[:1]:
        relay(p)
    work(hz - 1)
    for p in early[1:]:
        relay(p)
    work(0)
    rs_step(1)
    relay(hz - 1)
    if hy > 1:
        rs_step(2)
    relay(0)
    for step in range(3, hy + 1):
        rs_step(step)
    finish()
    rs_last()

    for t in (0, 1):
        for way in (0, 1):
            for step in range(1, hz + 1):
                z_copy(t, way, step, True).wait_send()
    for way in (0, 1):
        for step in range(1, hy + 1):
            y_copy(way, step, True).wait_send()
            for h in rs_halves(way, step):
                rs_copy(way, step, h).wait_send()
    for k in range(1, NZ):
        mt_copy(k, True).wait_send()
    for p in range(hz):
        for t in (0, 1):
            peers(lambda k: x_copy(p, t, k, True).wait_send())
        peers(lambda k: r_copy(p, k, True).wait_send())
        for s in (0, 1):
            if (p, s) != (0, 0):
                b_copy(p, s, True).wait_send()
    swaps[0].wait_send()
    for i in (1, 2):
        swaps[i].wait()


def exchange(tokens, upstream, meta, homec, flag, w_in, m_in, v_in):
    ny = lax.axis_size("dp")
    rows, width = tokens.shape
    part, both = w_in.shape
    hidden = both // 2
    ng = NX * NC
    hz, hy = NZ // 2, ny // 2
    chunk = 2 * CAP * ng
    lines = hz * chunk
    wide = width + LANES
    vmem = pl.BlockSpec(memory_space=pltpu.VMEM)
    any_ = pl.BlockSpec(memory_space=pl.ANY)
    dma = pltpu.SemaphoreType.DMA
    return pl.pallas_call(
        functools.partial(kernel, (ny, rows, width, hidden, wide)),
        name="exchange",
        out_shape=(
            jax.ShapeDtypeStruct((rows, width), BF16),
            jax.ShapeDtypeStruct((rows, LANES), F32),
            jax.ShapeDtypeStruct((part, both), F32),
            jax.ShapeDtypeStruct((part, both), BF16),
            jax.ShapeDtypeStruct((part, both), BF16),
            jax.ShapeDtypeStruct((part, both), BF16),
        ),
        in_specs=[vmem] * 6 + [any_] * 2,
        out_specs=(vmem,) * 4 + (any_,) * 2,
        scratch_shapes=[
            pltpu.VMEM((NZ * rows, width), BF16),
            pltpu.VMEM((NZ * rows, width), BF16),
            pltpu.VMEM((2, 2, chunk // 2 + chunk // 4, width), BF16),
            pltpu.VMEM((2, 2, chunk // 2 + chunk // 4, width), BF16),
            pltpu.VMEM((2, chunk // 2, width), BF16),
            pltpu.VMEM((NZ * 8, rows), F32),
            pltpu.VMEM((part, both), BF16),
            pltpu.VMEM((width, both), BF16),
            pltpu.VMEM((lines, width), BF16),
            pltpu.VMEM((lines, width), BF16),
            pltpu.VMEM((lines, width), BF16),
            pltpu.VMEM((lines, width), BF16),
            pltpu.VMEM((lines, hidden), BF16),
            pltpu.VMEM((lines, hidden), BF16),
            pltpu.VMEM((lines, wide), BF16),
            pltpu.VMEM((lines, wide), BF16),
            pltpu.VMEM((lines, wide), BF16),
            pltpu.VMEM((lines, wide), BF16),
            pltpu.VMEM((2, hy, 2, part, hidden), BF16),
            pltpu.VMEM((2, hy, 2, part, hidden), BF16),
            dma((2, 2, hz)), dma((2, 2, hz)),
            dma((NZ - 1,)), dma((NZ - 1,)),
            dma((3,)), dma((3,)),
            dma((2, hy)), dma((2, hy)),
            dma((2, hz, ng - 1)), dma((2, hz, ng - 1)),
            dma((hz, ng - 1)), dma((hz, ng - 1)),
            dma((hz, 2)), dma((hz, 2)),
            dma((2, hy, 2)), dma((2, hy, 2)),
            dma((1,)),
        ],
        compiler_params=pltpu.CompilerParams(
            collective_id=0, has_side_effects=True, vmem_limit_bytes=60 * 1024 * 1024
        ),
    )(tokens, upstream, meta, homec, flag, w_in, m_in, v_in)


def adam_update(weights, first, second, grad):
    m_next = 0.9 * first.astype(F32) + 0.1 * grad
    v_next = 0.999 * second.astype(F32) + 0.001 * grad * grad
    update = m_next / corr_one / (jnp.sqrt(v_next / corr_two) + 1e-08)
    w_old = weights.astype(F32)
    w_next = w_old - 0.001 * (update + 0.1 * w_old)
    return w_next.astype(BF16), m_next.astype(BF16), v_next.astype(BF16)


def shards(
    tokens,
    upstream,
    expert_ids,
    route_weight,
    placement,
    swap_pair,
    expert_state,
    first_moment,
    second_moment,
):
    lanes_count = lax.axis_size("expert")
    half = lanes_count // 2
    rows, top = expert_ids.shape
    both = expert_state.shape[2]
    halves = jnp.arange(half, dtype=jnp.int32)
    own_index = lax.axis_index("expert")
    own_flag = jnp.sum(jnp.where(halves == own_index % half, swap_pair, 0))
    match_half = (placement % half)[:, None] == halves[None, :]
    moved = jnp.sum(jnp.where(match_half, swap_pair[None, :], 0), 1)
    home = jnp.where(moved == 1, placement ^ half, placement)
    homec = jnp.broadcast_to(home.astype(F32)[:, None], (lanes_count, rows))
    flag = jnp.broadcast_to(own_flag.astype(F32), (8, both))
    meta = jnp.concatenate(
        [expert_ids.T.astype(F32), route_weight.T.astype(F32), jnp.zeros((8 - 2 * top, rows), F32)], 0
    )
    token_grad, weighted, grad, w_sel, m_got, v_got = exchange(
        tokens, upstream, meta, homec, flag, expert_state[0], first_moment[0], second_moment[0]
    )
    weight_grad = (weighted[:, :top] / route_weight.astype(F32)).astype(BF16)
    swapped = own_flag == 1
    m_sel = jnp.where(swapped, m_got, first_moment[0])
    v_sel = jnp.where(swapped, v_got, second_moment[0])
    w_new, m_new, v_new = adam_update(w_sel, m_sel, v_sel, grad)
    return (token_grad, weight_grad, w_new[None], m_new[None], v_new[None])


def solution(mesh):
    in_specs = (
        P(("expert", "dp"), None),
        P(("expert", "dp"), None),
        P(("expert", "dp"), None),
        P(("expert", "dp"), None),
        P(),
        P(),
        P("expert", "dp", None),
        P("expert", "dp", None),
        P("expert", "dp", None),
    )
    out_specs = (
        P(("expert", "dp"), None),
        P(("expert", "dp"), None),
        P("expert", "dp", None),
        P("expert", "dp", None),
        P("expert", "dp", None),
    )
    return jax.shard_map(shards, mesh=mesh, in_specs=in_specs, out_specs=out_specs, check_vma=False)
```

```python
import functools
import math

import jax
import jax.numpy as jnp
from jax import lax
from jax.experimental import pallas as pl
from jax.experimental.pallas import tpu as pltpu
from jax.sharding import PartitionSpec as P

corr_one = 1.0 - math.exp(1000.0 * math.log(0.9))
corr_two = 1.0 - math.exp(1000.0 * math.log(0.999))

NX, NZ, NC = 4, 8, 2
CAP = 8
LANES = 128
MESH = pl.DeviceIdType.MESH
F32 = jnp.float32
BF16 = jnp.bfloat16


def iota(shape, dim):
    return lax.broadcasted_iota(jnp.int32, shape, dim)


def tiles(total, tile, body):
    if total <= tile:
        body(0)
        return

    def step(i, carry):
        body(pl.multiple_of(i * tile, tile))
        return carry

    lax.fori_loop(0, total // tile, step, 0)


def kernel(
    sizes,
    tok, up, ids, gate, place_row, swap_row, w_in, m_in, v_in,
    tg, dwo, grad, w_sel, flag, m_got, v_got,
    xa, ya, p3, r3, r4, mt, w_got, wfull, sx, sy, rx, ry, act_all, dh_all,
    dxs, dr, sr, fr, rs_send, rs_recv,
    z_send, z_recv, mt_send, mt_recv, sw_send, sw_recv, y_send, y_recv,
    x_send, x_recv, r_send, r_recv, b_send, b_recv, rs_ssem, rs_rsem, local_sem,
):
    ny, rows, width, hidden, wide = sizes
    ng = NX * NC
    hz, hy = NZ // 2, ny // 2
    chunk = 2 * CAP * ng
    part = width // ny
    e = lax.axis_index("expert")
    d = lax.axis_index("dp")
    c = lax.rem(e, NC)
    z = lax.rem(e // NC, NZ)
    x = e // (NC * NZ)
    g = x * NC + c

    def zdev(k):
        return {"expert": (x * NZ + lax.rem(z + k + NZ, NZ)) * NC + c}

    def gdev(k):
        return {"expert": (lax.div(k, NC) * NZ + z) * NC + lax.rem(k, NC)}

    def ydev(k):
        return {"dp": lax.rem(d + k + ny, ny)}

    def remote(src, dst, ssem, rsem, dev):
        return pltpu.make_async_remote_copy(
            src_ref=src, dst_ref=dst, send_sem=ssem, recv_sem=rsem, device_id=dev, device_id_type=MESH
        )

    barrier = pltpu.get_barrier_semaphore()
    for k in range(1, NZ):
        pl.semaphore_signal(barrier, inc=1, device_id=zdev(k), device_id_type=MESH)
    for k in range(1, ng):
        pl.semaphore_signal(barrier, inc=1, device_id=gdev(lax.rem(g + k, ng)), device_id_type=MESH)
    for k in (1, -1):
        pl.semaphore_signal(barrier, inc=1, device_id=ydev(k), device_id_type=MESH)
    pl.semaphore_wait(barrier, NZ - 1 + ng - 1 + 2)

    own = (tok, up)
    every = (xa, ya)

    side_rows = CAP * ng
    split = side_rows // 2

    def z_copy(t, way, step, sending):
        sign = 1 if way == 0 else -1
        sems = z_send.at[t, way, step - 1], z_recv.at[t, way, step - 1]
        if step == hz:
            return remote(
                r3.at[t, way, pl.ds(side_rows, split)], r4.at[t, pl.ds(way * split, split)], *sems, zdev(sign)
            )
        if step == hz - 1:
            return remote(p3.at[t, way], r3.at[t, way], *sems, zdev(sign))
        back = step - 1 if sending else step
        block = lax.rem(z - sign * back + 2 * NZ, NZ)
        dst = every[t].at[pl.ds(pl.multiple_of(block * rows, rows), rows)]
        return remote(own[t] if step == 1 else dst, dst, *sems, zdev(sign))

    def z_start(t, step):
        for way in (0, 1):
            z_copy(t, way, step, True).start()

    def z_wait(t, step):
        for way in (0, 1):
            z_copy(t, way, step, False).wait_recv()

    half = NX * NZ * NC // 2
    partner = {"expert": lax.rem(e + half, 2 * half)}
    swaps = [
        remote(src, dst, sw_send.at[i], sw_recv.at[i], partner)
        for i, (src, dst) in enumerate(((w_in, w_got), (m_in, m_got), (v_in, v_got)))
    ]

    def y_copy(way, step, sending):
        sign = 1 if way == 0 else -1
        back = step - 1 if sending else step
        block = lax.rem(d - sign * back + 2 * ny, ny)
        start = pl.multiple_of(block * part, part)
        low, size = (0, part) if step < hy else (way * (part // 2), part // 2)
        ref = wfull.at[pl.ds(start + low, size)]
        return remote(ref, ref, y_send.at[way, step - 1], y_recv.at[way, step - 1], ydev(sign))

    def y_start(step):
        for way in (0, 1):
            y_copy(way, step, True).start()

    def y_wait(step):
        for way in (0, 1):
            y_copy(way, step, False).wait_recv()

    def mt_copy(k, sending):
        block = z if sending else lax.rem(z - k + NZ, NZ)
        ref = mt.at[pl.ds(pl.multiple_of(block * 8, 8), 8)]
        return remote(ref, ref, mt_send.at[k - 1], mt_recv.at[k - 1], zdev(k))

    def positions():
        experts = place_row.shape[1]
        pairs = experts // 2
        spread = jnp.where(iota((experts, experts), 0) == iota((experts, experts), 1), place_row[...], 0)
        place = jnp.sum(spread.astype(F32), 1, keepdims=True).astype(jnp.int32)
        low = jnp.where(place >= pairs, place - pairs, place)
        trade = jnp.where(iota((experts, pairs), 1) == low, swap_row[...], 0)
        moved = jnp.sum(trade.astype(F32), 1, keepdims=True) == 1.0
        home = jnp.where(moved, jnp.where(place >= pairs, place - pairs, place + pairs), place).astype(F32)
        mine = jnp.where(iota((8, pairs), 1) == lax.rem(e, pairs), swap_row[...], 0)
        flag[...] = jnp.broadcast_to(jnp.sum(mine.astype(F32), 1, keepdims=True), flag.shape)
        each = iota((experts, rows), 0)
        one0, one1 = ids[0:1, :] == each, ids[1:2, :] == each
        named = jnp.where(one0 | one1, 1.0, 0.0).astype(BF16)
        before = jnp.where(iota((rows, rows), 0) < iota((rows, rows), 1), 1.0, 0.0).astype(BF16)
        spot = home * CAP + jnp.dot(named, before, preferred_element_type=F32)
        pos0 = jnp.sum(jnp.where(one0, spot, 0.0), 0, keepdims=True)
        pos1 = jnp.sum(jnp.where(one1, spot, 0.0), 0, keepdims=True)
        line = iota((8, rows), 0)
        gates = gate[...].astype(F32)
        tile = jnp.where(line == 2, gates[0:1, :], gates[1:2, :])
        tile = jnp.where(line == 0, pos0, jnp.where(line == 1, pos1, tile))
        mt[pl.ds(pl.multiple_of(z * 8, 8), 8), :] = tile

    def sources(p):
        if p == 0:
            return z, lax.rem(z + hz, NZ)
        return lax.rem(z + p, NZ), lax.rem(z - p + NZ, NZ)

    def hot_rows(block, want, t):
        tile = mt[pl.ds(pl.multiple_of(block * 8, 8), 8), :]
        want = want.astype(F32)
        hit0, hit1 = tile[0:1, :] == want, tile[1:2, :] == want
        if t == 0:
            hot = jnp.where(hit0 | hit1, 1.0, 0.0)
        else:
            hot = jnp.where(hit0, tile[2:3, :], 0.0) + jnp.where(hit1, tile[3:4, :], 0.0)
        return hot.astype(BF16)

    def pack_ahead(t):
        lines = side_rows + split
        line = iota((lines, rows), 0)
        for way in (0, 1):
            sign = 1 if way == 0 else -1
            block = lax.rem(z - sign * (hz - 2) + NZ, NZ)
            later = line >= side_rows
            inner = jnp.where(later, line - side_rows + way * split, line)
            group, slot = inner // CAP, inner % CAP
            near, far = lax.rem(z + sign + NZ, NZ), lax.rem(z + 2 * sign + NZ, NZ)
            plane = jnp.where(later, far, near)
            hot = hot_rows(block, (((group // NC) * NZ + plane) * NC + group % NC) * CAP + slot, t)
            start = pl.multiple_of(block * rows, rows)

            def body(at):
                cols = pl.ds(at, min(512, width))
                p3[t, way, :, cols] = jnp.dot(
                    hot, every[t][pl.ds(start, rows), cols], preferred_element_type=F32
                ).astype(BF16)

            tiles(width, 512, body)

    def pack(p, t):
        line = iota((chunk, rows), 0)
        group, side, slot = line // (2 * CAP), (line // CAP) % 2, line % CAP
        aim = (((group // NC) * NZ + z) * NC + group % NC) * CAP + slot
        few = iota((chunk, side_rows), 0)
        spot = (few // (2 * CAP)) * CAP + few % CAP
        few_side = (few // CAP) % 2
        hots, lefts = [], []
        for s, block in enumerate(sources(p)):
            if p == hz - 1 or (p == 0 and s == 1):
                hit = (iota((chunk, side_rows), 1) == spot) & (few_side == s)
                hots.append(jnp.where(hit, 1.0, 0.0).astype(BF16))
                lefts.append(r4.at[t] if p == 0 else r3.at[t, 1 - s, pl.ds(0, side_rows)])
            else:
                hots.append(hot_rows(block, jnp.where(side == s, aim, -1), t))
                lefts.append(every[t].at[pl.ds(pl.multiple_of(block * rows, rows), rows)])
        out, got = ((sx, rx), (sy, ry))[t]
        mine = pl.ds(pl.multiple_of(p * chunk + g * 2 * CAP, 2 * CAP), 2 * CAP)

        def body(start):
            cols = pl.ds(start, min(512, width))
            packed = jnp.dot(hots[0], lefts[0][:, cols], preferred_element_type=F32)
            packed += jnp.dot(hots[1], lefts[1][:, cols], preferred_element_type=F32)
            out[pl.ds(p * chunk, chunk), cols] = packed.astype(BF16)

        tiles(width, 512, body)
        got[mine, :] = out[mine, :]

    def x_copy(p, t, k, sending):
        other = lax.rem(g + k, ng) if sending else lax.rem(g - k + ng, ng)
        src, dst = ((sx, rx), (sy, ry))[t]
        there = pl.ds(pl.multiple_of(p * chunk + other * 2 * CAP, 2 * CAP), 2 * CAP)
        here = pl.ds(pl.multiple_of(p * chunk + g * 2 * CAP, 2 * CAP), 2 * CAP)
        if sending:
            return remote(src.at[there], dst.at[here], x_send.at[t, p, k - 1], x_recv.at[t, p, k - 1], gdev(other))
        return remote(src.at[here], dst.at[there], x_send.at[t, p, k - 1], x_recv.at[t, p, k - 1], gdev(other))

    def peers(body):
        def step(k, carry):
            body(k)
            return carry

        lax.fori_loop(1, ng, step, 0)

    def x_start(p, t):
        peers(lambda k: x_copy(p, t, k, True).start())

    def x_wait(p, t):
        peers(lambda k: x_copy(p, t, k, False).wait_recv())

    def compute(p):
        at = pl.ds(p * chunk, chunk)
        hid = jnp.dot(rx[at, :], wfull[:, 0:hidden], preferred_element_type=F32)
        sig = 1.0 / (1.0 + jnp.exp(-hid))
        act = (hid * sig).astype(BF16)
        back = jnp.dot(ry[at, :], wfull[:, hidden:], preferred_element_type=F32)
        dh = (back * (sig * (1.0 + hid * (1.0 - sig)))).astype(BF16)
        act_all[at, :] = act
        dh_all[at, :] = dh
        weighted = jnp.sum(act.astype(F32) * back, 1, keepdims=True)
        dxs[at, width:] = jnp.broadcast_to(weighted, (chunk, LANES)).astype(BF16)

        def body(start):
            tile = wfull[pl.ds(start, min(512, width)), 0:hidden]
            dx = lax.dot_general(dh_all[at, :], tile, (((1,), (1,)), ((), ())), preferred_element_type=F32)
            dxs[at, pl.ds(start, min(512, width))] = dx.astype(BF16)

        tiles(width, 512, body)
        mine = pl.ds(pl.multiple_of(p * chunk + g * 2 * CAP, 2 * CAP), 2 * CAP)
        dr[mine, :] = dxs[mine, :]

    def r_copy(p, k, sending):
        other = lax.rem(g + k, ng) if sending else lax.rem(g - k + ng, ng)
        there = pl.ds(pl.multiple_of(p * chunk + other * 2 * CAP, 2 * CAP), 2 * CAP)
        here = pl.ds(pl.multiple_of(p * chunk + g * 2 * CAP, 2 * CAP), 2 * CAP)
        if sending:
            return remote(dxs.at[there], dr.at[here], r_send.at[p, k - 1], r_recv.at[p, k - 1], gdev(other))
        return remote(dxs.at[here], dr.at[there], r_send.at[p, k - 1], r_recv.at[p, k - 1], gdev(other))

    def r_start(p):
        peers(lambda k: r_copy(p, k, True).start())

    def b_copy(p, s, sending):
        away = hz if p == 0 else (p if s == 0 else -p)
        block = z if sending else lax.rem(z - away + NZ, NZ)
        src = sr.at[pl.ds((2 * p + s) * side_rows, side_rows)]
        dst = fr.at[pl.ds(pl.multiple_of(block * side_rows, side_rows), side_rows)]
        return remote(src, dst, b_send.at[p, s], b_recv.at[p, s], zdev(away))

    def r_wait(p):
        peers(lambda k: r_copy(p, k, False).wait_recv())

    def relay(p):
        r_wait(p)
        to, frm = iota((chunk, chunk), 0), iota((chunk, chunk), 1)
        side, group, slot = to // side_rows, (to // CAP) % ng, to % CAP
        move = jnp.where(frm == group * 2 * CAP + side * CAP + slot, 1.0, 0.0).astype(BF16)

        def body(start, size=min(512, width)):
            cols = pl.ds(start, size)
            moved = jnp.dot(move, dr[pl.ds(p * chunk, chunk), cols], preferred_element_type=F32)
            sr[pl.ds(p * chunk, chunk), cols] = moved.astype(BF16)

        tiles(width, 512, body)
        body(width, LANES)
        if p == 0:
            fr[pl.ds(pl.multiple_of(z * side_rows, side_rows), side_rows), :] = sr[0:side_rows, :]
            b_copy(0, 1, True).start()
        else:
            for s in (0, 1):
                b_copy(p, s, True).start()

    def own_part(block, h):
        cols = pl.ds(pl.multiple_of(block * part, part), part)
        left, right = ((rx, dh_all), (ry, act_all))[h]
        return lax.dot_general(
            left[:, cols], right[...], (((0,), (0,)), ((), ())), preferred_element_type=F32
        )

    def rs_copy(way, step, h):
        sign = 1 if way == 0 else -1
        return remote(
            rs_send.at[way, step - 1, h], rs_recv.at[way, step - 1, h],
            rs_ssem.at[way, step - 1, h], rs_rsem.at[way, step - 1, h], ydev(sign),
        )

    def rs_halves(way, step):
        return (way,) if step == 1 else (0, 1)

    def rs_step(step):
        for h in (0, 1):
            for way in (0, 1):
                if h not in rs_halves(way, step):
                    continue
                sign = 1 if way == 0 else -1
                block = lax.rem(d + sign * (hy + 1 - step) + ny, ny)
                total = own_part(block, h)
                if step > 1 and h in rs_halves(way, step - 1):
                    rs_copy(way, step - 1, h).wait_recv()
                    total += rs_recv[way, step - 2, h].astype(F32)
                rs_send[way, step - 1, h] = total.astype(BF16)
                rs_copy(way, step, h).start()

    def rs_last():
        for h in (0, 1):
            total = own_part(d, h)
            for way in (0, 1):
                if h in rs_halves(way, hy):
                    rs_copy(way, hy, h).wait_recv()
                    total += rs_recv[way, hy - 1, h].astype(F32)
            grad[:, h * hidden : (h + 1) * hidden] = total

    def finish():
        for p in range(hz):
            for s in (0, 1):
                if (p, s) != (0, 0):
                    b_copy(p, s, False).wait_recv()
        tile = mt[pl.ds(pl.multiple_of(z * 8, 8), 8), :]
        lines = side_rows * NZ
        line = iota((lines, rows), 0)
        plane, group, slot = line // side_rows, (line // CAP) % ng, line % CAP
        want = ((((group // NC) * NZ + plane) * NC + group % NC) * CAP + slot).astype(F32)
        hit0, hit1 = tile[0:1, :] == want, tile[1:2, :] == want
        both = jnp.where(hit0 | hit1, 1.0, 0.0).astype(BF16)
        dims = (((0,), (0,)), ((), ()))

        def body(start):
            cols = pl.ds(start, min(512, width))
            tg[:, cols] = lax.dot_general(both, fr[:, cols], dims, preferred_element_type=F32).astype(BF16)

        tiles(width, 512, body)
        for k, hit in enumerate((hit0, hit1)):
            sums = lax.dot_general(
                fr[:, width:], jnp.where(hit, 1.0, 0.0).astype(BF16), dims, preferred_element_type=F32
            )
            dwo[k : k + 1, :] = (sums[0:1, :] / tile[2 + k : 3 + k, :]).astype(BF16)

    def metas_in():
        for k in range(1, NZ):
            mt_copy(k, False).wait_recv()

    def state_in():
        swaps[0].wait_recv()
        here = pl.ds(pl.multiple_of(d * part, part), part)
        chosen = jnp.where(flag[0:1, :] == 1.0, w_got[...].astype(F32), w_in[...].astype(F32)).astype(BF16)
        wfull[here, :] = chosen
        w_sel[...] = chosen
        y_start(1)

    y_step = [0]

    def y_next():
        step = y_step[0] = y_step[0] + 1
        if step <= hy:
            y_wait(step)
            if step < hy:
                y_start(step + 1)

    def metas_out():
        positions()
        for k in range(1, NZ):
            mt_copy(k, True).start()

    def own_rows():
        xa[pl.ds(pl.multiple_of(z * rows, rows), rows), :] = tok[...]
        ya[pl.ds(pl.multiple_of(z * rows, rows), rows), :] = up[...]

    def send_on(t, step):
        if step == hz - 1:
            pack_ahead(t)
        z_start(t, step)

    def dispatch(p, t):
        pack(p, t)
        x_start(p, t)

    def work(p):
        for t in (0, 1):
            x_wait(p, t)
        compute(p)

    swaps[0].start()
    if hz > 2:
        z_start(0, 1)
        metas_out()
        z_start(1, 1)
        own_rows()
    else:
        metas_out()
        own_rows()
        metas_in()
        send_on(0, 1)
        send_on(1, 1)
        state_in()
        swaps[1].start()
        swaps[2].start()
    for step in range(1, hz - 1):
        z_wait(0, step)
        if step == 2:
            send_on(0, step + 1)
            y_next()
        else:
            send_on(0, step + 1)
            state_in()
            swaps[1].start()
        z_wait(1, step)
        send_on(1, step + 1)
        if step == 1:
            y_next()
            metas_in()
        dispatch(step, 0)
        dispatch(step, 1)
        if step == 1:
            swaps[2].start()
        else:
            y_next()
    early = list(range(1, hz - 1))
    z_wait(0, hz - 1)
    z_start(0, hz)
    dispatch(hz - 1, 0)
    while y_step[0] < hy:
        y_next()
    if early:
        work(early[0])
    z_wait(1, hz - 1)
    z_start(1, hz)
    dispatch(hz - 1, 1)
    for p in early[1:]:
        work(p)
        r_start(p)
    for t in (0, 1):
        z_wait(t, hz)
        dispatch(0, t)
    for p in early[1:]:
        relay(p)
    work(hz - 1)
    r_start(hz - 1)
    work(0)
    r_start(0)
    for p in early[:1]:
        r_start(p)
    rs_step(1)
    relay(hz - 1)
    if hy > 1:
        rs_step(2)
    relay(0)
    for p in early[:1]:
        relay(p)
    for step in range(3, hy + 1):
        rs_step(step)
    finish()
    rs_last()

    for t in (0, 1):
        for way in (0, 1):
            for step in range(1, hz + 1):
                z_copy(t, way, step, True).wait_send()
    for way in (0, 1):
        for step in range(1, hy + 1):
            y_copy(way, step, True).wait_send()
            for h in rs_halves(way, step):
                rs_copy(way, step, h).wait_send()
    for k in range(1, NZ):
        mt_copy(k, True).wait_send()
    for p in range(hz):
        for t in (0, 1):
            peers(lambda k: x_copy(p, t, k, True).wait_send())
        peers(lambda k: r_copy(p, k, True).wait_send())
        for s in (0, 1):
            if (p, s) != (0, 0):
                b_copy(p, s, True).wait_send()
    swaps[0].wait_send()
    for i in (1, 2):
        swaps[i].wait()


def exchange(tokens, upstream, ids, gate, place, swap, w_in, m_in, v_in):
    ny = lax.axis_size("dp")
    rows, width = tokens.shape
    part, both = w_in.shape
    hidden = both // 2
    ng = NX * NC
    hz, hy = NZ // 2, ny // 2
    chunk = 2 * CAP * ng
    lines = hz * chunk
    wide = width + LANES
    vmem = pl.BlockSpec(memory_space=pltpu.VMEM)
    any_ = pl.BlockSpec(memory_space=pl.ANY)
    dma = pltpu.SemaphoreType.DMA
    return pl.pallas_call(
        functools.partial(kernel, (ny, rows, width, hidden, wide)),
        name="exchange",
        out_shape=(
            jax.ShapeDtypeStruct((rows, width), BF16),
            jax.ShapeDtypeStruct((2, rows), BF16),
            jax.ShapeDtypeStruct((part, both), F32),
            jax.ShapeDtypeStruct((part, both), BF16),
            jax.ShapeDtypeStruct((8, both), F32),
            jax.ShapeDtypeStruct((part, both), BF16),
            jax.ShapeDtypeStruct((part, both), BF16),
        ),
        in_specs=[vmem] * 7 + [any_] * 2,
        out_specs=(vmem,) * 5 + (any_,) * 2,
        scratch_shapes=[
            pltpu.VMEM((NZ * rows, width), BF16),
            pltpu.VMEM((NZ * rows, width), BF16),
            pltpu.VMEM((2, 2, chunk // 2 + chunk // 4, width), BF16),
            pltpu.VMEM((2, 2, chunk // 2 + chunk // 4, width), BF16),
            pltpu.VMEM((2, chunk // 2, width), BF16),
            pltpu.VMEM((NZ * 8, rows), F32),
            pltpu.VMEM((part, both), BF16),
            pltpu.VMEM((width, both), BF16),
            pltpu.VMEM((lines, width), BF16),
            pltpu.VMEM((lines, width), BF16),
            pltpu.VMEM((lines, width), BF16),
            pltpu.VMEM((lines, width), BF16),
            pltpu.VMEM((lines, hidden), BF16),
            pltpu.VMEM((lines, hidden), BF16),
            pltpu.VMEM((lines, wide), BF16),
            pltpu.VMEM((lines, wide), BF16),
            pltpu.VMEM((lines, wide), BF16),
            pltpu.VMEM((lines, wide), BF16),
            pltpu.VMEM((2, hy, 2, part, hidden), BF16),
            pltpu.VMEM((2, hy, 2, part, hidden), BF16),
            dma((2, 2, hz)), dma((2, 2, hz)),
            dma((NZ - 1,)), dma((NZ - 1,)),
            dma((3,)), dma((3,)),
            dma((2, hy)), dma((2, hy)),
            dma((2, hz, ng - 1)), dma((2, hz, ng - 1)),
            dma((hz, ng - 1)), dma((hz, ng - 1)),
            dma((hz, 2)), dma((hz, 2)),
            dma((2, hy, 2)), dma((2, hy, 2)),
            dma((1,)),
        ],
        compiler_params=pltpu.CompilerParams(
            collective_id=0, has_side_effects=True, vmem_limit_bytes=60 * 1024 * 1024
        ),
    )(tokens, upstream, ids, gate, place, swap, w_in, m_in, v_in)


def adam_update(weights, first, second, grad):
    m_next = 0.9 * first.astype(F32) + 0.1 * grad
    v_next = 0.999 * second.astype(F32) + 0.001 * grad * grad
    update = m_next / corr_one / (jnp.sqrt(v_next / corr_two) + 1e-08)
    w_old = weights.astype(F32)
    w_next = w_old - 0.001 * (update + 0.1 * w_old)
    return w_next.astype(BF16), m_next.astype(BF16), v_next.astype(BF16)


def shards(
    tokens,
    upstream,
    expert_ids,
    route_weight,
    placement,
    swap_pair,
    expert_state,
    first_moment,
    second_moment,
):
    token_grad, weight_grad, grad, w_sel, flag, m_got, v_got = exchange(
        tokens, upstream, expert_ids.T, route_weight.T, placement[None], swap_pair[None],
        expert_state[0], first_moment[0], second_moment[0],
    )
    swapped = flag[0:1] == 1.0
    m_sel = jnp.where(swapped, m_got, first_moment[0])
    v_sel = jnp.where(swapped, v_got, second_moment[0])
    w_new, m_new, v_new = adam_update(w_sel, m_sel, v_sel, grad)
    return (token_grad, weight_grad.T, w_new[None], m_new[None], v_new[None])


def solution(mesh):
    in_specs = (
        P(("expert", "dp"), None),
        P(("expert", "dp"), None),
        P(("expert", "dp"), None),
        P(("expert", "dp"), None),
        P(),
        P(),
        P("expert", "dp", None),
        P("expert", "dp", None),
        P("expert", "dp", None),
    )
    out_specs = (
        P(("expert", "dp"), None),
        P(("expert", "dp"), None),
        P("expert", "dp", None),
        P("expert", "dp", None),
        P("expert", "dp", None),
    )
    return jax.shard_map(shards, mesh=mesh, in_specs=in_specs, out_specs=out_specs, check_vma=False)
```

```python
import functools
import math

import jax
import jax.numpy as jnp
from jax import lax
from jax.experimental import pallas as pl
from jax.experimental.pallas import tpu as pltpu
from jax.sharding import PartitionSpec as P

corr_one = 1.0 - math.exp(1000.0 * math.log(0.9))
corr_two = 1.0 - math.exp(1000.0 * math.log(0.999))

NX, NZ, NC = 4, 8, 2
CAP = 8
LANES = 128
MESH = pl.DeviceIdType.MESH
F32 = jnp.float32
BF16 = jnp.bfloat16


def iota(shape, dim):
    return lax.broadcasted_iota(jnp.int32, shape, dim)


def tiles(total, tile, body):
    if total <= tile:
        body(0)
        return

    def step(i, carry):
        body(pl.multiple_of(i * tile, tile))
        return carry

    lax.fori_loop(0, total // tile, step, 0)


def kernel(
    sizes,
    tok, up, ids, gate, place_row, swap_row, w_in, m_in, v_in,
    tg, dwo, grad, w_sel, flag, m_got, v_got,
    xa, ya, p3, r3, r4, mt, w_got, wfull, sx, sy, rx, ry, act_all, dh_all,
    dxs, dr, sr, fr, rs_send, rs_recv,
    z_send, z_recv, mt_send, mt_recv, sw_send, sw_recv, y_send, y_recv,
    x_send, x_recv, r_send, r_recv, b_send, b_recv, rs_ssem, rs_rsem, local_sem,
):
    ny, rows, width, hidden, wide = sizes
    ng = NX * NC
    hz, hy = NZ // 2, ny // 2
    chunk = 2 * CAP * ng
    part = width // ny
    e = lax.axis_index("expert")
    d = lax.axis_index("dp")
    c = lax.rem(e, NC)
    z = lax.rem(e // NC, NZ)
    x = e // (NC * NZ)
    g = x * NC + c

    def zdev(k):
        return {"expert": (x * NZ + lax.rem(z + k + NZ, NZ)) * NC + c}

    def gdev(k):
        return {"expert": (lax.div(k, NC) * NZ + z) * NC + lax.rem(k, NC)}

    def ydev(k):
        return {"dp": lax.rem(d + k + ny, ny)}

    def remote(src, dst, ssem, rsem, dev):
        return pltpu.make_async_remote_copy(
            src_ref=src, dst_ref=dst, send_sem=ssem, recv_sem=rsem, device_id=dev, device_id_type=MESH
        )

    barrier = pltpu.get_barrier_semaphore()
    for k in range(1, NZ):
        pl.semaphore_signal(barrier, inc=1, device_id=zdev(k), device_id_type=MESH)
    for k in range(1, ng):
        pl.semaphore_signal(barrier, inc=1, device_id=gdev(lax.rem(g + k, ng)), device_id_type=MESH)
    for k in (1, -1):
        pl.semaphore_signal(barrier, inc=1, device_id=ydev(k), device_id_type=MESH)
    pl.semaphore_wait(barrier, NZ - 1 + ng - 1 + 2)

    own = (tok, up)
    every = (xa, ya)

    side_rows = CAP * ng
    split = side_rows // 2

    def z_copy(t, way, step, sending):
        sign = 1 if way == 0 else -1
        sems = z_send.at[t, way, step - 1], z_recv.at[t, way, step - 1]
        if step == hz:
            return remote(
                r3.at[t, way, pl.ds(side_rows, split)], r4.at[t, pl.ds(way * split, split)], *sems, zdev(sign)
            )
        if step == hz - 1:
            return remote(p3.at[t, way], r3.at[t, way], *sems, zdev(sign))
        back = step - 1 if sending else step
        block = lax.rem(z - sign * back + 2 * NZ, NZ)
        dst = every[t].at[pl.ds(pl.multiple_of(block * rows, rows), rows)]
        return remote(own[t] if step == 1 else dst, dst, *sems, zdev(sign))

    def z_start(t, step):
        for way in (0, 1):
            z_copy(t, way, step, True).start()

    def z_wait(t, step):
        for way in (0, 1):
            z_copy(t, way, step, False).wait_recv()

    half = NX * NZ * NC // 2
    partner = {"expert": lax.rem(e + half, 2 * half)}
    swaps = [
        remote(src, dst, sw_send.at[i], sw_recv.at[i], partner)
        for i, (src, dst) in enumerate(((w_in, w_got), (m_in, m_got), (v_in, v_got)))
    ]

    def y_copy(way, step, sending):
        sign = 1 if way == 0 else -1
        back = step - 1 if sending else step
        block = lax.rem(d - sign * back + 2 * ny, ny)
        start = pl.multiple_of(block * part, part)
        low, size = (0, part) if step < hy else (way * (part // 2), part // 2)
        ref = wfull.at[pl.ds(start + low, size)]
        return remote(ref, ref, y_send.at[way, step - 1], y_recv.at[way, step - 1], ydev(sign))

    def y_start(step):
        for way in (0, 1):
            y_copy(way, step, True).start()

    def y_wait(step):
        for way in (0, 1):
            y_copy(way, step, False).wait_recv()

    def mt_copy(k, sending):
        block = z if sending else lax.rem(z - k + NZ, NZ)
        ref = mt.at[pl.ds(pl.multiple_of(block * 8, 8), 8)]
        return remote(ref, ref, mt_send.at[k - 1], mt_recv.at[k - 1], zdev(k))

    def positions():
        experts = place_row.shape[1]
        pairs = experts // 2
        spread = jnp.where(iota((experts, experts), 0) == iota((experts, experts), 1), place_row[...], 0)
        place = jnp.sum(spread.astype(F32), 1, keepdims=True).astype(jnp.int32)
        low = jnp.where(place >= pairs, place - pairs, place)
        trade = jnp.where(iota((experts, pairs), 1) == low, swap_row[...], 0)
        moved = jnp.sum(trade.astype(F32), 1, keepdims=True) == 1.0
        home = jnp.where(moved, jnp.where(place >= pairs, place - pairs, place + pairs), place).astype(F32)
        mine = jnp.where(iota((8, pairs), 1) == lax.rem(e, pairs), swap_row[...], 0)
        flag[...] = jnp.broadcast_to(jnp.sum(mine.astype(F32), 1, keepdims=True), flag.shape)
        each = iota((experts, rows), 0)
        one0, one1 = ids[0:1, :] == each, ids[1:2, :] == each
        named = jnp.where(one0 | one1, 1.0, 0.0).astype(BF16)
        before = jnp.where(iota((rows, rows), 0) < iota((rows, rows), 1), 1.0, 0.0).astype(BF16)
        spot = home * CAP + jnp.dot(named, before, preferred_element_type=F32)
        pos0 = jnp.sum(jnp.where(one0, spot, 0.0), 0, keepdims=True)
        pos1 = jnp.sum(jnp.where(one1, spot, 0.0), 0, keepdims=True)
        line = iota((8, rows), 0)
        gates = gate[...].astype(F32)
        tile = jnp.where(line == 2, gates[0:1, :], gates[1:2, :])
        tile = jnp.where(line == 0, pos0, jnp.where(line == 1, pos1, tile))
        mt[pl.ds(pl.multiple_of(z * 8, 8), 8), :] = tile

    def sources(p):
        if p == 0:
            return z, lax.rem(z + hz, NZ)
        return lax.rem(z + p, NZ), lax.rem(z - p + NZ, NZ)

    def hot_rows(block, want, t):
        tile = mt[pl.ds(pl.multiple_of(block * 8, 8), 8), :]
        want = want.astype(F32)
        hit0, hit1 = tile[0:1, :] == want, tile[1:2, :] == want
        if t == 0:
            hot = jnp.where(hit0 | hit1, 1.0, 0.0)
        else:
            hot = jnp.where(hit0, tile[2:3, :], 0.0) + jnp.where(hit1, tile[3:4, :], 0.0)
        return hot.astype(BF16)

    def pack_ahead(t):
        lines = side_rows + split
        line = iota((lines, rows), 0)
        for way in (0, 1):
            sign = 1 if way == 0 else -1
            block = lax.rem(z - sign * (hz - 2) + NZ, NZ)
            later = line >= side_rows
            inner = jnp.where(later, line - side_rows + way * split, line)
            group, slot = inner // CAP, inner % CAP
            near, far = lax.rem(z + sign + NZ, NZ), lax.rem(z + 2 * sign + NZ, NZ)
            plane = jnp.where(later, far, near)
            hot = hot_rows(block, (((group // NC) * NZ + plane) * NC + group % NC) * CAP + slot, t)
            start = pl.multiple_of(block * rows, rows)

            def body(at):
                cols = pl.ds(at, min(512, width))
                p3[t, way, :, cols] = jnp.dot(
                    hot, every[t][pl.ds(start, rows), cols], preferred_element_type=F32
                ).astype(BF16)

            tiles(width, 512, body)

    def pack(p, t):
        line = iota((chunk, rows), 0)
        group, side, slot = line // (2 * CAP), (line // CAP) % 2, line % CAP
        aim = (((group // NC) * NZ + z) * NC + group % NC) * CAP + slot
        few = iota((chunk, side_rows), 0)
        spot = (few // (2 * CAP)) * CAP + few % CAP
        few_side = (few // CAP) % 2
        hots, lefts = [], []
        for s, block in enumerate(sources(p)):
            if p == hz - 1 or (p == 0 and s == 1):
                hit = (iota((chunk, side_rows), 1) == spot) & (few_side == s)
                hots.append(jnp.where(hit, 1.0, 0.0).astype(BF16))
                lefts.append(r4.at[t] if p == 0 else r3.at[t, 1 - s, pl.ds(0, side_rows)])
            else:
                hots.append(hot_rows(block, jnp.where(side == s, aim, -1), t))
                lefts.append(every[t].at[pl.ds(pl.multiple_of(block * rows, rows), rows)])
        out, got = ((sx, rx), (sy, ry))[t]
        mine = pl.ds(pl.multiple_of(p * chunk + g * 2 * CAP, 2 * CAP), 2 * CAP)

        def body(start):
            cols = pl.ds(start, min(512, width))
            packed = jnp.dot(hots[0], lefts[0][:, cols], preferred_element_type=F32)
            packed += jnp.dot(hots[1], lefts[1][:, cols], preferred_element_type=F32)
            out[pl.ds(p * chunk, chunk), cols] = packed.astype(BF16)

        tiles(width, 512, body)
        got[mine, :] = out[mine, :]

    def x_copy(p, t, k, sending):
        other = lax.rem(g + k, ng) if sending else lax.rem(g - k + ng, ng)
        src, dst = ((sx, rx), (sy, ry))[t]
        there = pl.ds(pl.multiple_of(p * chunk + other * 2 * CAP, 2 * CAP), 2 * CAP)
        here = pl.ds(pl.multiple_of(p * chunk + g * 2 * CAP, 2 * CAP), 2 * CAP)
        if sending:
            return remote(src.at[there], dst.at[here], x_send.at[t, p, k - 1], x_recv.at[t, p, k - 1], gdev(other))
        return remote(src.at[here], dst.at[there], x_send.at[t, p, k - 1], x_recv.at[t, p, k - 1], gdev(other))

    def peers(body):
        def step(k, carry):
            body(k)
            return carry

        lax.fori_loop(1, ng, step, 0)

    def x_start(p, t):
        peers(lambda k: x_copy(p, t, k, True).start())

    def x_wait(p, t):
        peers(lambda k: x_copy(p, t, k, False).wait_recv())

    def compute(p):
        at = pl.ds(p * chunk, chunk)
        hid = jnp.dot(rx[at, :], wfull[:, 0:hidden], preferred_element_type=F32)
        sig = 1.0 / (1.0 + jnp.exp(-hid))
        act = (hid * sig).astype(BF16)
        back = jnp.dot(ry[at, :], wfull[:, hidden:], preferred_element_type=F32)
        dh = (back * (sig * (1.0 + hid * (1.0 - sig)))).astype(BF16)
        act_all[at, :] = act
        dh_all[at, :] = dh
        weighted = jnp.sum(act.astype(F32) * back, 1, keepdims=True)
        dxs[at, width:] = jnp.broadcast_to(weighted, (chunk, LANES)).astype(BF16)

        def body(start):
            tile = wfull[pl.ds(start, min(512, width)), 0:hidden]
            dx = lax.dot_general(dh_all[at, :], tile, (((1,), (1,)), ((), ())), preferred_element_type=F32)
            dxs[at, pl.ds(start, min(512, width))] = dx.astype(BF16)

        tiles(width, 512, body)
        mine = pl.ds(pl.multiple_of(p * chunk + g * 2 * CAP, 2 * CAP), 2 * CAP)
        dr[mine, :] = dxs[mine, :]

    def r_copy(p, k, sending):
        other = lax.rem(g + k, ng) if sending else lax.rem(g - k + ng, ng)
        there = pl.ds(pl.multiple_of(p * chunk + other * 2 * CAP, 2 * CAP), 2 * CAP)
        here = pl.ds(pl.multiple_of(p * chunk + g * 2 * CAP, 2 * CAP), 2 * CAP)
        if sending:
            return remote(dxs.at[there], dr.at[here], r_send.at[p, k - 1], r_recv.at[p, k - 1], gdev(other))
        return remote(dxs.at[here], dr.at[there], r_send.at[p, k - 1], r_recv.at[p, k - 1], gdev(other))

    def r_start(p):
        peers(lambda k: r_copy(p, k, True).start())

    def b_copy(p, s, sending):
        away = hz if p == 0 else (p if s == 0 else -p)
        block = z if sending else lax.rem(z - away + NZ, NZ)
        src = sr.at[pl.ds((2 * p + s) * side_rows, side_rows)]
        dst = fr.at[pl.ds(pl.multiple_of(block * side_rows, side_rows), side_rows)]
        return remote(src, dst, b_send.at[p, s], b_recv.at[p, s], zdev(away))

    def r_wait(p):
        peers(lambda k: r_copy(p, k, False).wait_recv())

    def relay(p):
        r_wait(p)
        to, frm = iota((chunk, chunk), 0), iota((chunk, chunk), 1)
        side, group, slot = to // side_rows, (to // CAP) % ng, to % CAP
        move = jnp.where(frm == group * 2 * CAP + side * CAP + slot, 1.0, 0.0).astype(BF16)

        def body(start, size=min(512, width)):
            cols = pl.ds(start, size)
            moved = jnp.dot(move, dr[pl.ds(p * chunk, chunk), cols], preferred_element_type=F32)
            sr[pl.ds(p * chunk, chunk), cols] = moved.astype(BF16)

        tiles(width, 512, body)
        body(width, LANES)
        if p == 0:
            fr[pl.ds(pl.multiple_of(z * side_rows, side_rows), side_rows), :] = sr[0:side_rows, :]
            b_copy(0, 1, True).start()
        else:
            for s in (0, 1):
                b_copy(p, s, True).start()

    def own_part(block, h):
        cols = pl.ds(pl.multiple_of(block * part, part), part)
        left, right = ((rx, dh_all), (ry, act_all))[h]
        return lax.dot_general(
            left[:, cols], right[...], (((0,), (0,)), ((), ())), preferred_element_type=F32
        )

    def rs_copy(way, step, h):
        sign = 1 if way == 0 else -1
        return remote(
            rs_send.at[way, step - 1, h], rs_recv.at[way, step - 1, h],
            rs_ssem.at[way, step - 1, h], rs_rsem.at[way, step - 1, h], ydev(sign),
        )

    def rs_halves(way, step):
        return (way,) if step == 1 else (0, 1)

    def rs_step(step):
        for h in (0, 1):
            for way in (0, 1):
                if h not in rs_halves(way, step):
                    continue
                sign = 1 if way == 0 else -1
                block = lax.rem(d + sign * (hy + 1 - step) + ny, ny)
                total = own_part(block, h)
                if step > 1 and h in rs_halves(way, step - 1):
                    rs_copy(way, step - 1, h).wait_recv()
                    total += rs_recv[way, step - 2, h].astype(F32)
                rs_send[way, step - 1, h] = total.astype(BF16)
                rs_copy(way, step, h).start()

    def rs_last():
        for h in (0, 1):
            total = own_part(d, h)
            for way in (0, 1):
                if h in rs_halves(way, hy):
                    rs_copy(way, hy, h).wait_recv()
                    total += rs_recv[way, hy - 1, h].astype(F32)
            grad[:, h * hidden : (h + 1) * hidden] = total

    def finish():
        for p in range(hz):
            for s in (0, 1):
                if (p, s) != (0, 0):
                    b_copy(p, s, False).wait_recv()
        tile = mt[pl.ds(pl.multiple_of(z * 8, 8), 8), :]
        lines = side_rows * NZ
        line = iota((lines, rows), 0)
        plane, group, slot = line // side_rows, (line // CAP) % ng, line % CAP
        want = ((((group // NC) * NZ + plane) * NC + group % NC) * CAP + slot).astype(F32)
        hit0, hit1 = tile[0:1, :] == want, tile[1:2, :] == want
        both = jnp.where(hit0 | hit1, 1.0, 0.0).astype(BF16)
        dims = (((0,), (0,)), ((), ()))

        def body(start):
            cols = pl.ds(start, min(512, width))
            tg[:, cols] = lax.dot_general(both, fr[:, cols], dims, preferred_element_type=F32).astype(BF16)

        tiles(width, 512, body)
        for k, hit in enumerate((hit0, hit1)):
            sums = lax.dot_general(
                fr[:, width:], jnp.where(hit, 1.0, 0.0).astype(BF16), dims, preferred_element_type=F32
            )
            dwo[k : k + 1, :] = (sums[0:1, :] / tile[2 + k : 3 + k, :]).astype(BF16)

    def metas_in():
        for k in range(1, NZ):
            mt_copy(k, False).wait_recv()

    def state_in():
        swaps[0].wait_recv()
        here = pl.ds(pl.multiple_of(d * part, part), part)
        chosen = jnp.where(flag[0:1, :] == 1.0, w_got[...].astype(F32), w_in[...].astype(F32)).astype(BF16)
        wfull[here, :] = chosen
        w_sel[...] = chosen
        y_start(1)

    y_step = [0]

    def y_next():
        step = y_step[0] = y_step[0] + 1
        if step <= hy:
            y_wait(step)
            if step < hy:
                y_start(step + 1)

    def metas_out():
        positions()
        for k in range(1, NZ):
            mt_copy(k, True).start()

    def own_rows():
        xa[pl.ds(pl.multiple_of(z * rows, rows), rows), :] = tok[...]
        ya[pl.ds(pl.multiple_of(z * rows, rows), rows), :] = up[...]

    def send_on(t, step):
        if step == hz - 1:
            pack_ahead(t)
        z_start(t, step)

    def dispatch(p, t):
        pack(p, t)
        x_start(p, t)

    def work(p):
        for t in (0, 1):
            x_wait(p, t)
        compute(p)

    swaps[0].start()
    z_start(0, 1)
    metas_out()
    own_rows()
    z_wait(0, 1)
    send_on(0, 2)
    send_on(1, 1)
    state_in()
    metas_in()
    dispatch(1, 0)
    swaps[1].start()
    z_wait(0, 2)
    send_on(0, 3)
    y_next()
    dispatch(2, 0)
    z_wait(1, 1)
    send_on(1, 2)
    dispatch(1, 1)
    swaps[2].start()
    y_next()
    z_wait(0, 3)
    send_on(0, 4)
    dispatch(3, 0)
    y_next()
    z_wait(1, 2)
    send_on(1, 3)
    dispatch(2, 1)
    z_wait(0, 4)
    dispatch(0, 0)
    while y_step[0] < hy:
        y_next()
    work(1)
    work(2)
    r_start(2)
    z_wait(1, 3)
    send_on(1, 4)
    dispatch(3, 1)
    z_wait(1, 4)
    dispatch(0, 1)
    relay(2)
    work(3)
    r_start(3)
    work(0)
    r_start(0)
    r_start(1)
    rs_step(1)
    relay(3)
    if hy > 1:
        rs_step(2)
    relay(0)
    relay(1)
    for step in range(3, hy + 1):
        rs_step(step)
    finish()
    rs_last()

    for t in (0, 1):
        for way in (0, 1):
            for step in range(1, hz + 1):
                z_copy(t, way, step, True).wait_send()
    for way in (0, 1):
        for step in range(1, hy + 1):
            y_copy(way, step, True).wait_send()
            for h in rs_halves(way, step):
                rs_copy(way, step, h).wait_send()
    for k in range(1, NZ):
        mt_copy(k, True).wait_send()
    for p in range(hz):
        for t in (0, 1):
            peers(lambda k: x_copy(p, t, k, True).wait_send())
        peers(lambda k: r_copy(p, k, True).wait_send())
        for s in (0, 1):
            if (p, s) != (0, 0):
                b_copy(p, s, True).wait_send()
    swaps[0].wait_send()
    for i in (1, 2):
        swaps[i].wait()


def exchange(tokens, upstream, ids, gate, place, swap, w_in, m_in, v_in):
    ny = lax.axis_size("dp")
    rows, width = tokens.shape
    part, both = w_in.shape
    hidden = both // 2
    ng = NX * NC
    hz, hy = NZ // 2, ny // 2
    chunk = 2 * CAP * ng
    lines = hz * chunk
    wide = width + LANES
    vmem = pl.BlockSpec(memory_space=pltpu.VMEM)
    any_ = pl.BlockSpec(memory_space=pl.ANY)
    dma = pltpu.SemaphoreType.DMA
    return pl.pallas_call(
        functools.partial(kernel, (ny, rows, width, hidden, wide)),
        name="exchange",
        out_shape=(
            jax.ShapeDtypeStruct((rows, width), BF16),
            jax.ShapeDtypeStruct((2, rows), BF16),
            jax.ShapeDtypeStruct((part, both), F32),
            jax.ShapeDtypeStruct((part, both), BF16),
            jax.ShapeDtypeStruct((8, both), F32),
            jax.ShapeDtypeStruct((part, both), BF16),
            jax.ShapeDtypeStruct((part, both), BF16),
        ),
        in_specs=[vmem] * 7 + [any_] * 2,
        out_specs=(vmem,) * 5 + (any_,) * 2,
        scratch_shapes=[
            pltpu.VMEM((NZ * rows, width), BF16),
            pltpu.VMEM((NZ * rows, width), BF16),
            pltpu.VMEM((2, 2, chunk // 2 + chunk // 4, width), BF16),
            pltpu.VMEM((2, 2, chunk // 2 + chunk // 4, width), BF16),
            pltpu.VMEM((2, chunk // 2, width), BF16),
            pltpu.VMEM((NZ * 8, rows), F32),
            pltpu.VMEM((part, both), BF16),
            pltpu.VMEM((width, both), BF16),
            pltpu.VMEM((lines, width), BF16),
            pltpu.VMEM((lines, width), BF16),
            pltpu.VMEM((lines, width), BF16),
            pltpu.VMEM((lines, width), BF16),
            pltpu.VMEM((lines, hidden), BF16),
            pltpu.VMEM((lines, hidden), BF16),
            pltpu.VMEM((lines, wide), BF16),
            pltpu.VMEM((lines, wide), BF16),
            pltpu.VMEM((lines, wide), BF16),
            pltpu.VMEM((lines, wide), BF16),
            pltpu.VMEM((2, hy, 2, part, hidden), BF16),
            pltpu.VMEM((2, hy, 2, part, hidden), BF16),
            dma((2, 2, hz)), dma((2, 2, hz)),
            dma((NZ - 1,)), dma((NZ - 1,)),
            dma((3,)), dma((3,)),
            dma((2, hy)), dma((2, hy)),
            dma((2, hz, ng - 1)), dma((2, hz, ng - 1)),
            dma((hz, ng - 1)), dma((hz, ng - 1)),
            dma((hz, 2)), dma((hz, 2)),
            dma((2, hy, 2)), dma((2, hy, 2)),
            dma((1,)),
        ],
        compiler_params=pltpu.CompilerParams(
            collective_id=0, has_side_effects=True, vmem_limit_bytes=60 * 1024 * 1024
        ),
    )(tokens, upstream, ids, gate, place, swap, w_in, m_in, v_in)


def adam_update(weights, first, second, grad):
    m_next = 0.9 * first.astype(F32) + 0.1 * grad
    v_next = 0.999 * second.astype(F32) + 0.001 * grad * grad
    update = m_next / corr_one / (jnp.sqrt(v_next / corr_two) + 1e-08)
    w_old = weights.astype(F32)
    w_next = w_old - 0.001 * (update + 0.1 * w_old)
    return w_next.astype(BF16), m_next.astype(BF16), v_next.astype(BF16)


def shards(
    tokens,
    upstream,
    expert_ids,
    route_weight,
    placement,
    swap_pair,
    expert_state,
    first_moment,
    second_moment,
):
    token_grad, weight_grad, grad, w_sel, flag, m_got, v_got = exchange(
        tokens, upstream, expert_ids.T, route_weight.T, placement[None], swap_pair[None],
        expert_state[0], first_moment[0], second_moment[0],
    )
    swapped = flag[0:1] == 1.0
    m_sel = jnp.where(swapped, m_got, first_moment[0])
    v_sel = jnp.where(swapped, v_got, second_moment[0])
    w_new, m_new, v_new = adam_update(w_sel, m_sel, v_sel, grad)
    return (token_grad, weight_grad.T, w_new[None], m_new[None], v_new[None])


def solution(mesh):
    in_specs = (
        P(("expert", "dp"), None),
        P(("expert", "dp"), None),
        P(("expert", "dp"), None),
        P(("expert", "dp"), None),
        P(),
        P(),
        P("expert", "dp", None),
        P("expert", "dp", None),
        P("expert", "dp", None),
    )
    out_specs = (
        P(("expert", "dp"), None),
        P(("expert", "dp"), None),
        P("expert", "dp", None),
        P("expert", "dp", None),
        P("expert", "dp", None),
    )
    return jax.shard_map(shards, mesh=mesh, in_specs=in_specs, out_specs=out_specs, check_vma=False)
```

```python
import functools
import math

import jax
import jax.numpy as jnp
from jax import lax
from jax.experimental import pallas as pl
from jax.experimental.pallas import tpu as pltpu
from jax.sharding import PartitionSpec as P

corr_one = 1.0 - math.exp(1000.0 * math.log(0.9))
corr_two = 1.0 - math.exp(1000.0 * math.log(0.999))

NX, NZ, NC = 4, 8, 2
CAP = 8
LANES = 128
MESH = pl.DeviceIdType.MESH
F32 = jnp.float32
BF16 = jnp.bfloat16


def iota(shape, dim):
    return lax.broadcasted_iota(jnp.int32, shape, dim)


def tiles(total, tile, body):
    if total <= tile:
        body(0)
        return

    def step(i, carry):
        body(pl.multiple_of(i * tile, tile))
        return carry

    lax.fori_loop(0, total // tile, step, 0)


def kernel(
    sizes,
    tok, up, ids, gate, place_row, swap_row, w_in, m_in, v_in,
    tg, dwo, grad, w_sel, flag, m_got, v_got,
    xa, ya, p3, r3, r4, mt, w_got, wfull, sx, sy, rx, ry, act_all, dh_all,
    dxs, dr, sr, fr, rs_send, rs_recv,
    z_send, z_recv, mt_send, mt_recv, sw_send, sw_recv, y_send, y_recv,
    x_send, x_recv, r_send, r_recv, b_send, b_recv, rs_ssem, rs_rsem, local_sem,
):
    ny, rows, width, hidden, wide = sizes
    ng = NX * NC
    hz, hy = NZ // 2, ny // 2
    chunk = 2 * CAP * ng
    part = width // ny
    e = lax.axis_index("expert")
    d = lax.axis_index("dp")
    c = lax.rem(e, NC)
    z = lax.rem(e // NC, NZ)
    x = e // (NC * NZ)
    g = x * NC + c

    def zdev(k):
        return {"expert": (x * NZ + lax.rem(z + k + NZ, NZ)) * NC + c}

    def gdev(k):
        return {"expert": (lax.div(k, NC) * NZ + z) * NC + lax.rem(k, NC)}

    def ydev(k):
        return {"dp": lax.rem(d + k + ny, ny)}

    def remote(src, dst, ssem, rsem, dev):
        return pltpu.make_async_remote_copy(
            src_ref=src, dst_ref=dst, send_sem=ssem, recv_sem=rsem, device_id=dev, device_id_type=MESH
        )

    barrier = pltpu.get_barrier_semaphore()
    for k in range(1, NZ):
        pl.semaphore_signal(barrier, inc=1, device_id=zdev(k), device_id_type=MESH)
    for k in range(1, ng):
        pl.semaphore_signal(barrier, inc=1, device_id=gdev(lax.rem(g + k, ng)), device_id_type=MESH)
    for k in (1, -1):
        pl.semaphore_signal(barrier, inc=1, device_id=ydev(k), device_id_type=MESH)
    pl.semaphore_wait(barrier, NZ - 1 + ng - 1 + 2)

    own = (tok, up)
    every = (xa, ya)

    side_rows = CAP * ng
    split = side_rows // 2

    def z_copy(t, way, step, sending):
        sign = 1 if way == 0 else -1
        sems = z_send.at[t, way, step - 1], z_recv.at[t, way, step - 1]
        if step == hz:
            return remote(
                r3.at[t, way, pl.ds(side_rows, split)], r4.at[t, pl.ds(way * split, split)], *sems, zdev(sign)
            )
        if step == hz - 1:
            return remote(p3.at[t, way], r3.at[t, way], *sems, zdev(sign))
        back = step - 1 if sending else step
        block = lax.rem(z - sign * back + 2 * NZ, NZ)
        dst = every[t].at[pl.ds(pl.multiple_of(block * rows, rows), rows)]
        return remote(own[t] if step == 1 else dst, dst, *sems, zdev(sign))

    def z_start(t, step):
        for way in (0, 1):
            z_copy(t, way, step, True).start()

    def z_wait(t, step):
        for way in (0, 1):
            z_copy(t, way, step, False).wait_recv()

    half = NX * NZ * NC // 2
    partner = {"expert": lax.rem(e + half, 2 * half)}
    swaps = [
        remote(src, dst, sw_send.at[i], sw_recv.at[i], partner)
        for i, (src, dst) in enumerate(((w_in, w_got), (m_in, m_got), (v_in, v_got)))
    ]

    def y_copy(way, step, sending):
        sign = 1 if way == 0 else -1
        back = step - 1 if sending else step
        block = lax.rem(d - sign * back + 2 * ny, ny)
        start = pl.multiple_of(block * part, part)
        low, size = (0, part) if step < hy else (way * (part // 2), part // 2)
        ref = wfull.at[pl.ds(start + low, size)]
        return remote(ref, ref, y_send.at[way, step - 1], y_recv.at[way, step - 1], ydev(sign))

    def y_start(step):
        for way in (0, 1):
            y_copy(way, step, True).start()

    def y_wait(step):
        for way in (0, 1):
            y_copy(way, step, False).wait_recv()

    def mt_copy(k, sending):
        block = z if sending else lax.rem(z - k + NZ, NZ)
        ref = mt.at[pl.ds(pl.multiple_of(block * 8, 8), 8)]
        return remote(ref, ref, mt_send.at[k - 1], mt_recv.at[k - 1], zdev(k))

    def positions():
        experts = place_row.shape[1]
        pairs = experts // 2
        spread = jnp.where(iota((experts, experts), 0) == iota((experts, experts), 1), place_row[...], 0)
        place = jnp.sum(spread.astype(F32), 1, keepdims=True).astype(jnp.int32)
        low = jnp.where(place >= pairs, place - pairs, place)
        trade = jnp.where(iota((experts, pairs), 1) == low, swap_row[...], 0)
        moved = jnp.sum(trade.astype(F32), 1, keepdims=True) == 1.0
        home = jnp.where(moved, jnp.where(place >= pairs, place - pairs, place + pairs), place).astype(F32)
        mine = jnp.where(iota((8, pairs), 1) == lax.rem(e, pairs), swap_row[...], 0)
        flag[...] = jnp.broadcast_to(jnp.sum(mine.astype(F32), 1, keepdims=True), flag.shape)
        each = iota((experts, rows), 0)
        one0, one1 = ids[0:1, :] == each, ids[1:2, :] == each
        named = jnp.where(one0 | one1, 1.0, 0.0).astype(BF16)
        before = jnp.where(iota((rows, rows), 0) < iota((rows, rows), 1), 1.0, 0.0).astype(BF16)
        spot = home * CAP + jnp.dot(named, before, preferred_element_type=F32)
        pos0 = jnp.sum(jnp.where(one0, spot, 0.0), 0, keepdims=True)
        pos1 = jnp.sum(jnp.where(one1, spot, 0.0), 0, keepdims=True)
        line = iota((8, rows), 0)
        gates = gate[...].astype(F32)
        tile = jnp.where(line == 2, gates[0:1, :], gates[1:2, :])
        tile = jnp.where(line == 0, pos0, jnp.where(line == 1, pos1, tile))
        mt[pl.ds(pl.multiple_of(z * 8, 8), 8), :] = tile

    def sources(p):
        if p == 0:
            return z, lax.rem(z + hz, NZ)
        return lax.rem(z + p, NZ), lax.rem(z - p + NZ, NZ)

    def hot_rows(block, want, t):
        tile = mt[pl.ds(pl.multiple_of(block * 8, 8), 8), :]
        want = want.astype(F32)
        hit0, hit1 = tile[0:1, :] == want, tile[1:2, :] == want
        if t == 0:
            hot = jnp.where(hit0 | hit1, 1.0, 0.0)
        else:
            hot = jnp.where(hit0, tile[2:3, :], 0.0) + jnp.where(hit1, tile[3:4, :], 0.0)
        return hot.astype(BF16)

    def pack_ahead(t):
        lines = side_rows + split
        line = iota((lines, rows), 0)
        for way in (0, 1):
            sign = 1 if way == 0 else -1
            block = lax.rem(z - sign * (hz - 2) + NZ, NZ)
            later = line >= side_rows
            inner = jnp.where(later, line - side_rows + way * split, line)
            group, slot = inner // CAP, inner % CAP
            near, far = lax.rem(z + sign + NZ, NZ), lax.rem(z + 2 * sign + NZ, NZ)
            plane = jnp.where(later, far, near)
            hot = hot_rows(block, (((group // NC) * NZ + plane) * NC + group % NC) * CAP + slot, t)
            start = pl.multiple_of(block * rows, rows)

            def body(at):
                cols = pl.ds(at, min(512, width))
                p3[t, way, :, cols] = jnp.dot(
                    hot, every[t][pl.ds(start, rows), cols], preferred_element_type=F32
                ).astype(BF16)

            tiles(width, 512, body)

    def pack(p, t):
        line = iota((chunk, rows), 0)
        group, side, slot = line // (2 * CAP), (line // CAP) % 2, line % CAP
        aim = (((group // NC) * NZ + z) * NC + group % NC) * CAP + slot
        few = iota((chunk, side_rows), 0)
        spot = (few // (2 * CAP)) * CAP + few % CAP
        few_side = (few // CAP) % 2
        hots, lefts = [], []
        for s, block in enumerate(sources(p)):
            if p == hz - 1 or (p == 0 and s == 1):
                hit = (iota((chunk, side_rows), 1) == spot) & (few_side == s)
                hots.append(jnp.where(hit, 1.0, 0.0).astype(BF16))
                lefts.append(r4.at[t] if p == 0 else r3.at[t, 1 - s, pl.ds(0, side_rows)])
            else:
                hots.append(hot_rows(block, jnp.where(side == s, aim, -1), t))
                lefts.append(every[t].at[pl.ds(pl.multiple_of(block * rows, rows), rows)])
        out, got = ((sx, rx), (sy, ry))[t]
        mine = pl.ds(pl.multiple_of(p * chunk + g * 2 * CAP, 2 * CAP), 2 * CAP)

        def body(start):
            cols = pl.ds(start, min(512, width))
            packed = jnp.dot(hots[0], lefts[0][:, cols], preferred_element_type=F32)
            packed += jnp.dot(hots[1], lefts[1][:, cols], preferred_element_type=F32)
            out[pl.ds(p * chunk, chunk), cols] = packed.astype(BF16)

        tiles(width, 512, body)
        got[mine, :] = out[mine, :]

    def x_copy(p, t, k, sending):
        other = lax.rem(g + k, ng) if sending else lax.rem(g - k + ng, ng)
        src, dst = ((sx, rx), (sy, ry))[t]
        there = pl.ds(pl.multiple_of(p * chunk + other * 2 * CAP, 2 * CAP), 2 * CAP)
        here = pl.ds(pl.multiple_of(p * chunk + g * 2 * CAP, 2 * CAP), 2 * CAP)
        if sending:
            return remote(src.at[there], dst.at[here], x_send.at[t, p, k - 1], x_recv.at[t, p, k - 1], gdev(other))
        return remote(src.at[here], dst.at[there], x_send.at[t, p, k - 1], x_recv.at[t, p, k - 1], gdev(other))

    def peers(body):
        def step(k, carry):
            body(k)
            return carry

        lax.fori_loop(1, ng, step, 0)

    def x_start(p, t):
        peers(lambda k: x_copy(p, t, k, True).start())

    def x_wait(p, t):
        peers(lambda k: x_copy(p, t, k, False).wait_recv())

    def compute(p):
        at = pl.ds(p * chunk, chunk)
        hid = jnp.dot(rx[at, :], wfull[:, 0:hidden], preferred_element_type=F32)
        sig = 1.0 / (1.0 + jnp.exp(-hid))
        act = (hid * sig).astype(BF16)
        back = jnp.dot(ry[at, :], wfull[:, hidden:], preferred_element_type=F32)
        dh = (back * (sig * (1.0 + hid * (1.0 - sig)))).astype(BF16)
        act_all[at, :] = act
        dh_all[at, :] = dh
        weighted = jnp.sum(act.astype(F32) * back, 1, keepdims=True)
        dxs[at, width:] = jnp.broadcast_to(weighted, (chunk, LANES)).astype(BF16)

        def body(start):
            tile = wfull[pl.ds(start, min(512, width)), 0:hidden]
            dx = lax.dot_general(dh_all[at, :], tile, (((1,), (1,)), ((), ())), preferred_element_type=F32)
            dxs[at, pl.ds(start, min(512, width))] = dx.astype(BF16)

        tiles(width, 512, body)
        mine = pl.ds(pl.multiple_of(p * chunk + g * 2 * CAP, 2 * CAP), 2 * CAP)
        dr[mine, :] = dxs[mine, :]

    def r_copy(p, k, sending):
        other = lax.rem(g + k, ng) if sending else lax.rem(g - k + ng, ng)
        there = pl.ds(pl.multiple_of(p * chunk + other * 2 * CAP, 2 * CAP), 2 * CAP)
        here = pl.ds(pl.multiple_of(p * chunk + g * 2 * CAP, 2 * CAP), 2 * CAP)
        if sending:
            return remote(dxs.at[there], dr.at[here], r_send.at[p, k - 1], r_recv.at[p, k - 1], gdev(other))
        return remote(dxs.at[here], dr.at[there], r_send.at[p, k - 1], r_recv.at[p, k - 1], gdev(other))

    def r_start(p):
        peers(lambda k: r_copy(p, k, True).start())

    def b_copy(p, s, sending):
        away = hz if p == 0 else (p if s == 0 else -p)
        block = z if sending else lax.rem(z - away + NZ, NZ)
        src = sr.at[pl.ds((2 * p + s) * side_rows, side_rows)]
        dst = fr.at[pl.ds(pl.multiple_of(block * side_rows, side_rows), side_rows)]
        return remote(src, dst, b_send.at[p, s], b_recv.at[p, s], zdev(away))

    def r_wait(p):
        peers(lambda k: r_copy(p, k, False).wait_recv())

    def relay(p):
        r_wait(p)
        to, frm = iota((chunk, chunk), 0), iota((chunk, chunk), 1)
        side, group, slot = to // side_rows, (to // CAP) % ng, to % CAP
        move = jnp.where(frm == group * 2 * CAP + side * CAP + slot, 1.0, 0.0).astype(BF16)

        def body(start, size=min(512, width)):
            cols = pl.ds(start, size)
            moved = jnp.dot(move, dr[pl.ds(p * chunk, chunk), cols], preferred_element_type=F32)
            sr[pl.ds(p * chunk, chunk), cols] = moved.astype(BF16)

        tiles(width, 512, body)
        body(width, LANES)
        if p == 0:
            fr[pl.ds(pl.multiple_of(z * side_rows, side_rows), side_rows), :] = sr[0:side_rows, :]
            b_copy(0, 1, True).start()
        else:
            for s in (0, 1):
                b_copy(p, s, True).start()

    def own_part(block, h):
        cols = pl.ds(pl.multiple_of(block * part, part), part)
        left, right = ((rx, dh_all), (ry, act_all))[h]
        return lax.dot_general(
            left[:, cols], right[...], (((0,), (0,)), ((), ())), preferred_element_type=F32
        )

    def rs_copy(way, step, h):
        sign = 1 if way == 0 else -1
        return remote(
            rs_send.at[way, step - 1, h], rs_recv.at[way, step - 1, h],
            rs_ssem.at[way, step - 1, h], rs_rsem.at[way, step - 1, h], ydev(sign),
        )

    def rs_halves(way, step):
        return (way,) if step == 1 else (0, 1)

    def rs_some(step, some):
        for way, h in some:
            sign = 1 if way == 0 else -1
            block = lax.rem(d + sign * (hy + 1 - step) + ny, ny)
            total = own_part(block, h)
            if step > 1 and h in rs_halves(way, step - 1):
                rs_copy(way, step - 1, h).wait_recv()
                total += rs_recv[way, step - 2, h].astype(F32)
            rs_send[way, step - 1, h] = total.astype(BF16)
            rs_copy(way, step, h).start()

    fresh, begun = ((0, 1), (1, 0)), ((0, 0), (1, 1))

    def rs_last():
        for h in (0, 1):
            total = own_part(d, h)
            for way in (0, 1):
                if h in rs_halves(way, hy):
                    rs_copy(way, hy, h).wait_recv()
                    total += rs_recv[way, hy - 1, h].astype(F32)
            grad[:, h * hidden : (h + 1) * hidden] = total

    def finish():
        for p in range(hz):
            for s in (0, 1):
                if (p, s) != (0, 0):
                    b_copy(p, s, False).wait_recv()
        tile = mt[pl.ds(pl.multiple_of(z * 8, 8), 8), :]
        lines = side_rows * NZ
        line = iota((lines, rows), 0)
        plane, group, slot = line // side_rows, (line // CAP) % ng, line % CAP
        want = ((((group // NC) * NZ + plane) * NC + group % NC) * CAP + slot).astype(F32)
        hit0, hit1 = tile[0:1, :] == want, tile[1:2, :] == want
        both = jnp.where(hit0 | hit1, 1.0, 0.0).astype(BF16)
        dims = (((0,), (0,)), ((), ()))

        def body(start):
            cols = pl.ds(start, min(512, width))
            tg[:, cols] = lax.dot_general(both, fr[:, cols], dims, preferred_element_type=F32).astype(BF16)

        tiles(width, 512, body)
        for k, hit in enumerate((hit0, hit1)):
            sums = lax.dot_general(
                fr[:, width:], jnp.where(hit, 1.0, 0.0).astype(BF16), dims, preferred_element_type=F32
            )
            dwo[k : k + 1, :] = (sums[0:1, :] / tile[2 + k : 3 + k, :]).astype(BF16)

    def metas_in():
        for k in range(1, NZ):
            mt_copy(k, False).wait_recv()

    def state_in():
        swaps[0].wait_recv()
        here = pl.ds(pl.multiple_of(d * part, part), part)
        chosen = jnp.where(flag[0:1, :] == 1.0, w_got[...].astype(F32), w_in[...].astype(F32)).astype(BF16)
        wfull[here, :] = chosen
        w_sel[...] = chosen
        y_start(1)

    y_step = [0]

    def y_next():
        step = y_step[0] = y_step[0] + 1
        if step <= hy:
            y_wait(step)
            if step < hy:
                y_start(step + 1)

    def metas_out():
        positions()
        for k in range(1, NZ):
            mt_copy(k, True).start()

    def own_rows():
        xa[pl.ds(pl.multiple_of(z * rows, rows), rows), :] = tok[...]
        ya[pl.ds(pl.multiple_of(z * rows, rows), rows), :] = up[...]

    def send_on(t, step):
        if step == hz - 1:
            pack_ahead(t)
        z_start(t, step)

    def dispatch(p, t):
        pack(p, t)
        x_start(p, t)

    def work(p):
        for t in (0, 1):
            x_wait(p, t)
        compute(p)

    swaps[0].start()
    z_start(0, 1)
    metas_out()
    own_rows()
    z_wait(0, 1)
    send_on(0, 2)
    send_on(1, 1)
    state_in()
    metas_in()
    dispatch(1, 0)
    swaps[1].start()
    z_wait(0, 2)
    send_on(0, 3)
    y_next()
    dispatch(2, 0)
    z_wait(1, 1)
    send_on(1, 2)
    dispatch(1, 1)
    swaps[2].start()
    y_next()
    z_wait(0, 3)
    send_on(0, 4)
    dispatch(3, 0)
    y_next()
    z_wait(1, 2)
    send_on(1, 3)
    dispatch(2, 1)
    z_wait(0, 4)
    dispatch(0, 0)
    while y_step[0] < hy:
        y_next()
    work(1)
    work(2)
    r_start(2)
    z_wait(1, 3)
    send_on(1, 4)
    dispatch(3, 1)
    z_wait(1, 4)
    dispatch(0, 1)
    relay(2)
    work(3)
    r_start(3)
    work(0)
    r_start(0)
    r_start(1)
    rs_some(1, begun)
    if hy > 1:
        rs_some(2, fresh)
    relay(3)
    if hy > 1:
        rs_some(2, begun)
    relay(0)
    for step in range(3, hy + 1):
        rs_some(step, fresh + begun)
        if step == 3:
            relay(1)
    if hy < 3:
        relay(1)
    finish()
    rs_last()

    for t in (0, 1):
        for way in (0, 1):
            for step in range(1, hz + 1):
                z_copy(t, way, step, True).wait_send()
    for way in (0, 1):
        for step in range(1, hy + 1):
            y_copy(way, step, True).wait_send()
            for h in rs_halves(way, step):
                rs_copy(way, step, h).wait_send()
    for k in range(1, NZ):
        mt_copy(k, True).wait_send()
    for p in range(hz):
        for t in (0, 1):
            peers(lambda k: x_copy(p, t, k, True).wait_send())
        peers(lambda k: r_copy(p, k, True).wait_send())
        for s in (0, 1):
            if (p, s) != (0, 0):
                b_copy(p, s, True).wait_send()
    swaps[0].wait_send()
    for i in (1, 2):
        swaps[i].wait()


def exchange(tokens, upstream, ids, gate, place, swap, w_in, m_in, v_in):
    ny = lax.axis_size("dp")
    rows, width = tokens.shape
    part, both = w_in.shape
    hidden = both // 2
    ng = NX * NC
    hz, hy = NZ // 2, ny // 2
    chunk = 2 * CAP * ng
    lines = hz * chunk
    wide = width + LANES
    vmem = pl.BlockSpec(memory_space=pltpu.VMEM)
    any_ = pl.BlockSpec(memory_space=pl.ANY)
    dma = pltpu.SemaphoreType.DMA
    return pl.pallas_call(
        functools.partial(kernel, (ny, rows, width, hidden, wide)),
        name="exchange",
        out_shape=(
            jax.ShapeDtypeStruct((rows, width), BF16),
            jax.ShapeDtypeStruct((2, rows), BF16),
            jax.ShapeDtypeStruct((part, both), F32),
            jax.ShapeDtypeStruct((part, both), BF16),
            jax.ShapeDtypeStruct((8, both), F32),
            jax.ShapeDtypeStruct((part, both), BF16),
            jax.ShapeDtypeStruct((part, both), BF16),
        ),
        in_specs=[vmem] * 7 + [any_] * 2,
        out_specs=(vmem,) * 5 + (any_,) * 2,
        scratch_shapes=[
            pltpu.VMEM((NZ * rows, width), BF16),
            pltpu.VMEM((NZ * rows, width), BF16),
            pltpu.VMEM((2, 2, chunk // 2 + chunk // 4, width), BF16),
            pltpu.VMEM((2, 2, chunk // 2 + chunk // 4, width), BF16),
            pltpu.VMEM((2, chunk // 2, width), BF16),
            pltpu.VMEM((NZ * 8, rows), F32),
            pltpu.VMEM((part, both), BF16),
            pltpu.VMEM((width, both), BF16),
            pltpu.VMEM((lines, width), BF16),
            pltpu.VMEM((lines, width), BF16),
            pltpu.VMEM((lines, width), BF16),
            pltpu.VMEM((lines, width), BF16),
            pltpu.VMEM((lines, hidden), BF16),
            pltpu.VMEM((lines, hidden), BF16),
            pltpu.VMEM((lines, wide), BF16),
            pltpu.VMEM((lines, wide), BF16),
            pltpu.VMEM((lines, wide), BF16),
            pltpu.VMEM((lines, wide), BF16),
            pltpu.VMEM((2, hy, 2, part, hidden), BF16),
            pltpu.VMEM((2, hy, 2, part, hidden), BF16),
            dma((2, 2, hz)), dma((2, 2, hz)),
            dma((NZ - 1,)), dma((NZ - 1,)),
            dma((3,)), dma((3,)),
            dma((2, hy)), dma((2, hy)),
            dma((2, hz, ng - 1)), dma((2, hz, ng - 1)),
            dma((hz, ng - 1)), dma((hz, ng - 1)),
            dma((hz, 2)), dma((hz, 2)),
            dma((2, hy, 2)), dma((2, hy, 2)),
            dma((1,)),
        ],
        compiler_params=pltpu.CompilerParams(
            collective_id=0, has_side_effects=True, vmem_limit_bytes=60 * 1024 * 1024
        ),
    )(tokens, upstream, ids, gate, place, swap, w_in, m_in, v_in)


def adam_update(weights, first, second, grad):
    m_next = 0.9 * first.astype(F32) + 0.1 * grad
    v_next = 0.999 * second.astype(F32) + 0.001 * grad * grad
    update = m_next / corr_one / (jnp.sqrt(v_next / corr_two) + 1e-08)
    w_old = weights.astype(F32)
    w_next = w_old - 0.001 * (update + 0.1 * w_old)
    return w_next.astype(BF16), m_next.astype(BF16), v_next.astype(BF16)


def shards(
    tokens,
    upstream,
    expert_ids,
    route_weight,
    placement,
    swap_pair,
    expert_state,
    first_moment,
    second_moment,
):
    token_grad, weight_grad, grad, w_sel, flag, m_got, v_got = exchange(
        tokens, upstream, expert_ids.T, route_weight.T, placement[None], swap_pair[None],
        expert_state[0], first_moment[0], second_moment[0],
    )
    swapped = flag[0:1] == 1.0
    m_sel = jnp.where(swapped, m_got, first_moment[0])
    v_sel = jnp.where(swapped, v_got, second_moment[0])
    w_new, m_new, v_new = adam_update(w_sel, m_sel, v_sel, grad)
    return (token_grad, weight_grad.T, w_new[None], m_new[None], v_new[None])


def solution(mesh):
    in_specs = (
        P(("expert", "dp"), None),
        P(("expert", "dp"), None),
        P(("expert", "dp"), None),
        P(("expert", "dp"), None),
        P(),
        P(),
        P("expert", "dp", None),
        P("expert", "dp", None),
        P("expert", "dp", None),
    )
    out_specs = (
        P(("expert", "dp"), None),
        P(("expert", "dp"), None),
        P("expert", "dp", None),
        P("expert", "dp", None),
        P("expert", "dp", None),
    )
    return jax.shard_map(shards, mesh=mesh, in_specs=in_specs, out_specs=out_specs, check_vma=False)
```
